32 devices in a mesh: grp: 2 (over core), band: 16 (over z, y, x), lev: 1.
Axes of the slice: x: 2, y: 2, z: 4, core: 2. Of those that a mesh axis runs over, the one named last changes fastest.
Arguments:
- spectral: bfloat16 [64, 64, 256], P(('grp', 'band'), None, 'lev'), may hold values from -6 to 6
- synthesis: bfloat16 [64, 128, 64], P(('grp', 'band')), may hold values from -0.75 to 0.75
- analysis: bfloat16 [64, 64, 128], P(('grp', 'band')), may hold values from -0.5 to 0.5
- interp_weights: bfloat16 [8, 256, 512], replicated, may hold values from -0.25 to 0.25
- tube_source: int32 [8192, 1], replicated, may hold values from 0 to 31; in each aligned block of 256 rows (0 to 255, 256 to 511, ...) at most 16 rows name the same one
- tube_column: int32 [8192], replicated, may hold values from 0 to 47
- weight_ids: int32 [8192], replicated, may hold values from 0 to 7
- tube_state: float32 [4, 8192, 256], P(None, ('grp', 'band'), 'lev'), may hold values from -6 to 6
- collision: float32 [8192, 256], P(('grp', 'band'), 'lev'), may hold values from 0.1 to 2
- end_coupling: float32 [4, 8192], P(None, ('grp', 'band')), may hold values from 0.3 to 0.7
- block_inverse: float32 [4, 256, 256], P(None, 'lev'), may hold values from -0.08 to 1.2
Outputs:
- spectral_new: float32 [64, 64, 256], P(('grp', 'band'), None, 'lev')
- tube_new: float32 [4, 8192, 256], P(None, ('grp', 'band'), 'lev')
The draws below stay inside these ranges and needn't reach their ends.
Inputs may be any that keep to these rules, and one draw needn't show every extreme that they name: `tube_source`: among the 256 tubes of one device (aligned blocks of tube indices), no value appears more than 16 times, and some value appears exactly 16 times.
All inputs are finite; a program needn't handle non-finite values.
Results may differ from the reference program's by a relative error of at most 0.0049.
Values may be sent and summed in bfloat16 or wider, within the bound.
No kernel may reach another device: no remote copies, remote signals or barrier semaphores. Data moves between devices by JAX's collectives and lax.ppermute only.
A program may use at most 64 MiB of HBM per device.

```python
import math
import jax
import jax.numpy as jnp
import numpy as np
from jax import lax

LON = 192
M = 64
NN = 64
F = 4
CW = 16
NW = 8
SWEEPS = 4
LAT_DEV = 4
LEV_DEV = 32
PTS_DEV = 256
TUBES_DEV = 256
SEGS = 1
LAT = 128
LEV = 32
TUBES = 8192
PTS = 256
NLB = 12
CB_DEV = 48
K = 512
C = 256
N_GRP = 2
N_BAND = 16


def draw_block_inverse(key, part):
    diagonal = jax.random.uniform(jax.random.fold_in(key, 11), (F, SEGS, PTS_DEV), jnp.float32, 0.6, 1.2)
    coupled = jax.random.uniform(jax.random.fold_in(key, 12), (F, SEGS, PTS_DEV, PTS_DEV), jnp.float32, -0.08, 0.08)
    identity = jnp.eye(PTS_DEV, dtype=jnp.float32)
    matrix = coupled * (1.0 - identity) + diagonal[..., None] * identity
    return matrix.reshape(F, SEGS * PTS_DEV, PTS_DEV)


def touch_ends(values, rng, smallest, top_value):
    longest = values.shape.index(max(values.shape))
    spots = []
    for shift in (0, 1):
        where = [jax.random.randint(jax.random.fold_in(rng, axis), (), 0, length) for axis, length in enumerate(values.shape)]
        where[longest] = (where[longest] + shift) % values.shape[longest]
        spots.append(tuple(where))
    return values.at[spots[0]].set(smallest).at[spots[1]].set(top_value)


def shard_levels(stream_key, dims, pieces, smallest, largest):
    def one(dim, parts):
        draws = jax.random.uniform(jax.random.fold_in(jax.random.fold_in(stream_key, 6), dim), (parts,), jnp.float32, smallest / len(pieces), largest / len(pieces))
        return jnp.repeat(jnp.exp(draws), dims[dim] // parts).reshape((-1,) + (1,) * (len(dims) - dim - 1))

    gain = one(*pieces[0])
    for cut in pieces[1:]:
        gain = gain * one(*cut)
    return gain


def routed_block(stream_key, own, number, rows, count, top, most, skew):
    ranking = jax.random.permutation(stream_key, count)
    heavy_load, common = shares(count, rows * top, most, skew, True), shares(count, rows * top, most, skew, False)
    places = jnp.arange(count)

    def named(sizes, rotation):
        used = int((sizes > 0).sum())
        fixed = max(1, used // 4)
        passed = fixed + (places - fixed + rotation * (used - fixed)) % max(1, count - fixed)
        return jnp.zeros((count,), jnp.int32).at[ranking[jnp.where(places < fixed, places, passed)]].set(jnp.asarray(sizes, jnp.int32))

    sizes = jnp.where(number % 4 == 0, named(heavy_load, number // 4), named(common, number - number // 4 - 1))
    mixed = jax.random.permutation(jax.random.fold_in(own, 3), count)
    giver, sink = mixed[0:count // 2 * 2:2], mixed[1:count // 2 * 2:2]
    margin = jnp.minimum(sizes[giver] - 1, most - sizes[sink]) // 2
    margin = jnp.where((giver == ranking[0]) | (sink == ranking[0]) | (sizes[sink] == 0), 0, jnp.maximum(margin, 0))
    passed = jax.random.randint(jax.random.fold_in(own, 4), (count // 2,), 0, 1 << 20) % (margin + 1)
    sizes = sizes.at[giver].add(-passed).at[sink].add(passed)
    labels = jnp.searchsorted(jnp.cumsum(sizes), jnp.arange(rows * top), side="right").astype(jnp.int32)
    table = labels.reshape(top, rows).T
    table = table[jax.random.permutation(jax.random.fold_in(own, 1), rows)]
    rotation = jax.random.randint(jax.random.fold_in(own, 2), (rows, 1), 0, top)
    return jnp.take_along_axis(table, (jnp.arange(top)[None, :] + rotation) % top, axis=1)


def shares(amount, total, bound, skew, full):
    weights = [(1 << 20) // math.isqrt(grade ** skew) + 1 for grade in range(1, amount + 1)]
    largest = bound if full else min(bound, max(-(-total // amount), total * weights[0] // sum(weights)))
    least = 1 if total - largest >= amount - 1 else 0
    holding, spare = [largest] + [least] * (amount - 1), total - largest - least * (amount - 1)
    while spare > 0:
        movable = [i for i in range(1, amount) if holding[i] < largest] or [i for i in range(1, amount) if holding[i] < bound]
        pool, left = sum([weights[i] for i in movable]), spare
        for i in movable:
            more = min(bound - holding[i], max(1, left * weights[i] // pool), spare)
            holding[i] = holding[i] + more
            spare = spare - more
    return np.array(holding)


def scatter_about(key, shape, width, most, shards=(), held_as=jnp.bfloat16):
    result = jax.random.normal(key, shape, jnp.float32) * width
    if len(shards) > 0:
        result = shard_levels(key, shape, shards, -0.22, 0.18) * result
    return jnp.clip(result, min=-most, max=most).astype(held_as)


def setup_inputs(seed: int = 0) -> dict:
    splits = jax.random.split(jax.random.key(seed), 12)
    spectral = scatter_about(splits[0], (M, NN, C), 1.0, 6.0, ((0, 32),))
    synthesis = scatter_about(splits[1], (M, LAT, NN), NN ** -0.5, 0.75, ((0, 32),))
    analysis = scatter_about(splits[2], (M, NN, LAT), LAT ** -0.5, 0.5, ((0, 32),))
    interp_weights = scatter_about(splits[3], (NW, PTS_DEV, K), K ** -0.5, 0.25)
    tube_source_keys = jax.random.split(jax.random.fold_in(splits[4], 1), TUBES // TUBES_DEV)
    tube_source_turns = jax.random.permutation(jax.random.fold_in(splits[4], 3), TUBES // TUBES_DEV)
    tube_source = jax.vmap(lambda own, number: routed_block(jax.random.fold_in(splits[4], 2), own, number, TUBES_DEV, N_GRP * N_BAND, 1, 2 * TUBES_DEV // (N_GRP * N_BAND), 2))(tube_source_keys, tube_source_turns).reshape((TUBES, 1))
    tube_column = touch_ends(jax.random.randint(splits[5], (TUBES,), 0, CB_DEV), jax.random.fold_in(splits[5], 1), 0, CB_DEV - 1).astype(jnp.int32)
    weight_ids = touch_ends(jax.random.randint(splits[6], (TUBES,), 0, NW), jax.random.fold_in(splits[6], 1), 0, NW - 1).astype(jnp.int32)
    tube_state = scatter_about(splits[7], (F, TUBES, PTS), 1.0, 6.0, ((1, 32),), jnp.float32)
    collision = jnp.clip(jnp.exp(math.log(2.0) - 2.9957323 * jax.random.uniform(splits[8], (TUBES, PTS), jnp.float32) ** shard_levels(splits[8], (TUBES, PTS), ((0, 32),), -0.2, 0.2)), 0.1, 2.0)
    end_coupling = jnp.clip(0.3 + 0.39999998 * jax.random.uniform(splits[9], (F, TUBES), jnp.float32) ** shard_levels(splits[9], (F, TUBES), ((1, 32),), -0.2, 0.2), 0.3, 0.7)
    block_inverse = draw_block_inverse(jax.random.fold_in(splits[11], 71), 0)
    return dict(spectral=spectral, synthesis=synthesis, analysis=analysis, interp_weights=interp_weights, tube_source=tube_source, tube_column=tube_column, weight_ids=weight_ids, tube_state=tube_state, collision=collision, end_coupling=end_coupling, block_inverse=block_inverse)


def fourier_table(wavenumbers, points):
    index_grid = (jnp.arange(wavenumbers, dtype=jnp.int32)[:, None] * jnp.arange(points, dtype=jnp.int32)[None, :]) % points
    angles = index_grid.astype(jnp.float32) * (2.0 * math.pi / points)
    return jnp.stack([jnp.cos(angles), -jnp.sin(angles)], axis=1)


def reference(spectral, synthesis, analysis, interp_weights, tube_source, tube_column, weight_ids, tube_state, collision, end_coupling, block_inverse):
    sources = N_GRP * N_BAND
    highest = lax.Precision.HIGHEST
    fourier = jnp.einsum("mlj,mjc->mlc", synthesis.astype(jnp.float32), spectral.astype(jnp.float32), precision=highest).astype(jnp.bfloat16)
    table = fourier_table(M, LON)
    spectra = fourier.astype(jnp.float32).reshape(M, LAT, LEV, F, 2)
    grid = (jnp.einsum("mlzfr,mro->lfzo", spectra, table, precision=highest) * (M ** -0.5)).astype(jnp.bfloat16)
    blocks = grid.reshape(sources, LAT_DEV, F, SEGS, LEV_DEV, NLB, CW).transpose(3, 0, 1, 5, 2, 4, 6).reshape(SEGS, sources * CB_DEV, F, K)
    gid = tube_source[:, 0].astype(jnp.int32) * CB_DEV + tube_column.astype(jnp.int32)

    def interpolate(operands):
        chosen, targets = operands
        weight_rows = interp_weights[chosen].astype(jnp.float32)
        block_rows = blocks[:, targets].astype(jnp.float32)
        return jnp.einsum("tpk,stfk->ftsp", weight_rows, block_rows, precision=highest)

    grouped_weights = weight_ids.reshape(sources, TUBES_DEV)
    neutral = lax.map(interpolate, (grouped_weights, gid.reshape(sources, TUBES_DEV)))
    neutral = neutral.transpose(1, 0, 2, 3, 4).reshape(F, TUBES, PTS).astype(jnp.bfloat16)

    inverse = block_inverse.reshape(F, SEGS, PTS_DEV, PTS_DEV)

    def solve(vector):
        return jnp.einsum("fspq,ftsq->ftsp", inverse, vector, precision=highest)

    forcing = (tube_state + neutral.astype(jnp.float32)).reshape(F, TUBES, SEGS, PTS_DEV)
    state = solve(forcing)
    coupling = end_coupling[:, :, None]
    for sweep_index in range(SWEEPS):
        from_left = jnp.pad(state[:, :, :-1, -1], ((0, 0), (0, 0), (1, 0)))
        from_right = jnp.pad(state[:, :, 1:, 0], ((0, 0), (0, 0), (0, 1)))
        coupled = forcing.at[:, :, :, 0].add(coupling * from_left)
        coupled = coupled.at[:, :, :, -1].add(coupling * from_right)
        state = solve(coupled)
    tube_new = state.reshape(F, TUBES, PTS)

    drag = (collision[None, :, :] * (tube_new - neutral.astype(jnp.float32))).astype(jnp.bfloat16)
    drag_groups = drag.reshape(F, sources, TUBES_DEV, SEGS, PTS_DEV).transpose(1, 0, 2, 3, 4)

    def spread_back(operands):
        chosen, drag_rows = operands
        weight_rows = interp_weights[chosen].astype(jnp.float32)
        return jnp.einsum("tpk,ftsp->tsfk", weight_rows, drag_rows.astype(jnp.float32), precision=highest).astype(jnp.bfloat16)

    contrib = lax.map(spread_back, (grouped_weights, drag_groups))
    contrib = contrib.reshape(TUBES, SEGS, F, K).astype(jnp.float32)
    tend_blocks = jax.ops.segment_sum(contrib, gid, num_segments=sources * CB_DEV)
    tendency = tend_blocks.reshape(sources, LAT_DEV, NLB, SEGS, F, LEV_DEV, CW).transpose(0, 1, 4, 3, 5, 2, 6).reshape(LAT, F, LEV, LON)
    analysed = jnp.einsum("lfzo,mro->mlzfr", tendency, table, precision=highest) * (LON ** -0.5)
    analysed = analysed.reshape(M, LAT, C).astype(jnp.bfloat16)
    update = jnp.einsum("mjl,mlc->mjc", analysis.astype(jnp.float32), analysed.astype(jnp.float32), precision=highest)
    return spectral.astype(jnp.float32) + update, tube_new
```

```python
import math

import jax
import jax.numpy as jnp
import numpy as np
from jax import lax
from jax.experimental import pallas as pl
from jax.experimental.pallas import tpu as pltpu
from jax.sharding import PartitionSpec as P

LON = 192
SWEEPS = 4
BF = jnp.bfloat16
F32 = jnp.float32
I32 = jnp.int32


def dot(a, b):
    return jnp.dot(a, b, preferred_element_type=F32)


def dot_nt(a, b):
    return lax.dot_general(a, b, (((1,), (1,)), ((), ())), preferred_element_type=F32)


def split(x):
    high = x.astype(BF)
    return high, (x - high.astype(F32)).astype(BF)


def iota(shape, dim):
    return lax.broadcasted_iota(I32, shape, dim)


def onehot(mask):
    return mask.astype(F32).astype(BF)


class Plan:
    def __init__(self, sources, spectral, synthesis, weights, tube_state):
        self.sources = sources
        self.wave_local, self.latitudes, self.degrees = synthesis
        self.waves = self.wave_local * sources
        self.lat_local = self.latitudes // sources
        self.columns = spectral[2]
        self.fields, self.tubes, self.points = tube_state
        self.matrices, _, self.block = weights
        self.levels = self.columns // (2 * self.fields)
        self.width = self.block // self.levels
        self.lon_blocks = LON // self.width
        self.lon_pad = -(-self.lon_blocks // 16) * 16
        self.capacity = 2 * self.tubes // sources
        self.slots = sources * self.capacity
        self.chunk = self.wave_local * self.lat_local
        self.rows = sources * self.chunk
        self.cells = self.lat_local * self.lon_pad
        self.table = self.matrices * self.cells
        self.values = self.fields * self.points
        self.half = self.fields * self.levels


def column_order(plan, transposed):
    n = plan.columns
    natural, moved = (1, 0) if transposed else (0, 1)
    new = iota((n, n), moved)
    part, rest = new // plan.half, new % plan.half
    field, level = rest // plan.levels, rest % plan.levels
    return onehot((level * plan.fields + field) * 2 + part == iota((n, n), natural))


def regrouped_rows(plan, back):
    n = plan.rows
    new = iota((n, n), 0)
    first = plan.sources if back else plan.wave_local
    outer, rest = new // (first * plan.lat_local), new % (first * plan.lat_local)
    middle, last = rest // plan.lat_local, rest % plan.lat_local
    count = plan.wave_local if back else plan.sources
    return onehot((middle * count + outer) * plan.lat_local + last == iota((n, n), 1))


def fourier_tables(plan):
    wave = np.arange(plan.waves)
    lon = np.arange(LON)
    angle = 2.0 * math.pi * ((wave[:, None] * lon[None, :]) % LON) / LON
    full = np.stack([np.cos(angle), -np.sin(angle)], 0)
    full = full.reshape(2, plan.waves, plan.lon_blocks, plan.width)
    full = np.pad(full, ((0, 0), (0, 0), (0, plan.lon_pad - plan.lon_blocks), (0, 0)))
    forward = full.transpose(3, 2, 0, 1).reshape(plan.width * plan.lon_pad, 2 * plan.waves)
    high = forward.astype(BF)
    low = (forward - high.astype(np.float64)).astype(BF)
    synthesis = np.concatenate([high, low], 1)
    analysis = np.concatenate([high.T, low.T, high.T], 1)
    return jnp.asarray(synthesis), jnp.asarray(analysis)


def exchange(plan, array):
    shaped = array.reshape(plan.sources, array.shape[0] // plan.sources, array.shape[1])
    moved = lax.all_to_all(shaped, ("grp", "band"), split_axis=0, concat_axis=0, tiled=True)
    return moved.reshape(array.shape)


def synthesis_kernel(plan, spectral, synthesis, out):
    order = column_order(plan, False)
    parts = []
    for wave in range(plan.wave_local):
        moved = dot(spectral[wave], order).astype(BF)
        parts.append(dot(synthesis[wave], moved).astype(BF))
    stacked = jnp.concatenate(parts, 0)
    out[...] = dot(regrouped_rows(plan, False), stacked).astype(BF)


def routing_kernel(
    plan, me, owners, columns, weight_of, weights, weights_out, pick, pick_t, seat, seat_t
):
    here = me[0]
    sources, tubes, capacity, slots = plan.sources, plan.tubes, plan.capacity, plan.slots
    k = plan.block
    moved = iota((k, k), 1)
    reorder = onehot(
        (moved % plan.levels) * plan.width + moved // plan.levels == iota((k, k), 0)
    )
    for matrix in range(plan.matrices):
        rows = slice(matrix * plan.points, (matrix + 1) * plan.points)
        weights_out[rows, :] = dot(weights[matrix], reorder).astype(BF)

    mask = owners[...] == here
    before = onehot(iota((tubes, tubes), 0) < iota((tubes, tubes), 1))
    rank = dot(onehot(mask), before)
    rank = jnp.where(mask, rank, -1.0)
    column = columns[...]
    cell = column
    for step in range(1, plan.lat_local):
        late = (column >= step * plan.lon_blocks).astype(I32)
        cell = cell + late * (plan.lon_pad - plan.lon_blocks)
    cell = (cell + 1).astype(F32)
    matrix = weight_of[...].astype(F32)
    repeat = onehot(iota((slots, sources), 0) // capacity == iota((slots, sources), 1))
    rank_all = dot(repeat, rank.astype(BF))
    cell_all = dot(repeat, cell.astype(BF))
    matrix_all = dot(repeat, matrix.astype(BF))
    place = (iota((slots, tubes), 0) % capacity).astype(F32)
    chosen = rank_all == place
    cell_slot = jnp.where(chosen, cell_all, 0.0)
    matrix_slot = jnp.where(chosen, matrix_all, 0.0)
    entry = jnp.sum(cell_slot + matrix_slot * plan.cells, axis=1, keepdims=True)
    pick[...] = onehot(entry.astype(I32) - 1 == iota((slots, plan.table), 1))
    ones = jnp.ones((16, tubes), BF)
    entry_row = dot_nt(ones, cell_slot.astype(BF)) + dot_nt(
        ones, matrix_slot.astype(BF)
    ) * plan.cells
    entry_row = entry_row[0:1, :].astype(I32) - 1
    pick_t[...] = onehot(entry_row == iota((plan.table, slots), 0))

    mine = owners[pl.ds(here, 1), :]
    square = (tubes, tubes)
    down, across = iota(square, 0), iota(square, 1)
    mine_col = jnp.sum(jnp.where(down == across, mine, 0), axis=1, keepdims=True)
    same = mine_col == mine
    rank_row = jnp.sum((same & (down < across)).astype(I32), axis=0, keepdims=True)
    rank_col = jnp.sum((same & (across < down)).astype(I32), axis=1, keepdims=True)
    seat[...] = onehot(mine_col * capacity + rank_col == iota((tubes, slots), 1))
    seat_t[...] = onehot(mine * capacity + rank_row == iota((slots, tubes), 0))


def lane_masks(plan, rows):
    group = iota((rows, plan.half), 1) // plan.levels
    return [group == index for index in range(plan.fields)]


def chosen_lanes(plan, masks, pieces):
    result = pieces[0]
    for index in range(1, plan.fields):
        result = jnp.where(masks[index], pieces[index], result)
    return result


def rolled(plan, array, groups):
    groups = groups % plan.fields
    if groups == 0:
        return array
    return pltpu.roll(array, groups * plan.levels, axis=1)


def neutral_kernel(plan, arrived, table, weights, pick, out, blocks, outcomes):
    order = onehot(
        (iota((plan.rows, plan.rows), 0) % plan.waves) * plan.lat_local
        + iota((plan.rows, plan.rows), 0) // plan.waves
        == iota((plan.rows, plan.rows), 1)
    )
    by_lat = dot(order, arrived[...]).astype(BF)
    stacks = []
    for lat in range(plan.lat_local):
        rows = by_lat[lat * plan.waves : (lat + 1) * plan.waves, :]
        stacks.append(jnp.concatenate([rows[:, : plan.half], rows[:, plan.half :]], 0))
    spectra = jnp.concatenate(stacks, 1)
    spectra = jnp.concatenate([spectra, spectra], 0)
    grid = dot(table[...], spectra) * plan.waves ** (-0.5)
    masks = lane_masks(plan, plan.cells)
    per = plan.fields
    for step in range(plan.width // per):
        pieces = []
        for index in range(per):
            start = (step * per + index) * plan.lon_pad
            rows = grid[start : start + plan.lon_pad, :]
            pieces.append(
                jnp.concatenate(
                    [
                        rows[:, lat * plan.half : (lat + 1) * plan.half]
                        for lat in range(plan.lat_local)
                    ],
                    0,
                )
            )
        for field in range(plan.fields):
            turned = [rolled(plan, pieces[index], index - field) for index in range(per)]
            blocks[
                field * plan.cells : (field + 1) * plan.cells,
                step * plan.half : (step + 1) * plan.half,
            ] = chosen_lanes(plan, masks, turned).astype(BF)
    values = blocks[...]
    for matrix in range(plan.matrices):
        part = weights[matrix * plan.points : (matrix + 1) * plan.points, :]
        found = dot_nt(values, part).astype(BF)
        for field in range(plan.fields):
            outcomes[
                matrix * plan.cells : (matrix + 1) * plan.cells,
                field * plan.points : (field + 1) * plan.points,
            ] = found[field * plan.cells : (field + 1) * plan.cells, :]
    out[...] = dot(pick[...], outcomes[...]).astype(BF)


def tube_kernel(
    plan, arrived, seat, seat_t, tube_state, collision, inverse, state_out, out, drag
):
    neutral = dot(seat[...], arrived[...])
    for field in range(plan.fields):
        lanes = slice(field * plan.points, (field + 1) * plan.points)
        wind = neutral[:, lanes]
        force_high, force_low = split(tube_state[field] + wind)
        inverse_high, inverse_low = split(inverse[field])
        state = dot_nt(force_high, inverse_high) + (
            dot_nt(force_high, inverse_low) + dot_nt(force_low, inverse_high)
        )
        state_out[field] = state
        drag[:, lanes] = (collision[...] * (state - wind)).astype(BF)
    out[...] = dot(seat_t[...], drag[...]).astype(BF)


def tendency_kernel(plan, arrived, table, weights, pick_t, out, sums, spread):
    found = dot(pick_t[...], arrived[...]).astype(BF)
    for matrix in range(plan.matrices):
        for field in range(plan.fields):
            sums[
                field * plan.cells : (field + 1) * plan.cells,
                matrix * plan.points : (matrix + 1) * plan.points,
            ] = found[
                matrix * plan.cells : (matrix + 1) * plan.cells,
                field * plan.points : (field + 1) * plan.points,
            ]
    tendency = dot(sums[...], weights[...])
    masks = lane_masks(plan, plan.cells)
    per = plan.fields
    for step in range(plan.width // per):
        lanes = slice(step * plan.half, (step + 1) * plan.half)
        pieces = [
            tendency[field * plan.cells : (field + 1) * plan.cells, lanes]
            for field in range(plan.fields)
        ]
        for index in range(per):
            turned = [
                rolled(plan, pieces[field], field - index) for field in range(plan.fields)
            ]
            mixed = chosen_lanes(plan, masks, turned)
            start = (step * per + index) * plan.lon_pad
            for lat in range(plan.lat_local):
                spread[
                    start : start + plan.lon_pad, lat * plan.half : (lat + 1) * plan.half
                ] = mixed[lat * plan.lon_pad : (lat + 1) * plan.lon_pad, :]
    high, low = split(spread[...])
    analysed = dot(table[...], jnp.concatenate([high, high, low], 0)) * LON ** (-0.5)
    analysed = analysed.astype(BF)
    stacks = []
    for lat in range(plan.lat_local):
        lanes = analysed[:, lat * plan.half : (lat + 1) * plan.half]
        stacks.append(jnp.concatenate([lanes[: plan.waves], lanes[plan.waves :]], 1))
    stacked = jnp.concatenate(stacks, 0)
    new = iota((plan.rows, plan.rows), 0)
    order = onehot(
        (new % plan.lat_local) * plan.waves + new // plan.lat_local
        == iota((plan.rows, plan.rows), 1)
    )
    out[...] = dot(order, stacked).astype(BF)


def analysis_kernel(plan, arrived, analysis, spectral, out):
    grouped = dot(regrouped_rows(plan, True), arrived[...]).astype(BF)
    natural = dot(grouped, column_order(plan, True)).astype(BF)
    for wave in range(plan.wave_local):
        rows = natural[wave * plan.latitudes : (wave + 1) * plan.latitudes, :]
        out[wave] = spectral[wave].astype(F32) + dot(analysis[wave], rows)


def call(plan, kernel, outs, operands, scratch=(), smem=0, flops=0):
    vmem = pl.BlockSpec(memory_space=pltpu.VMEM)
    in_specs = [
        pl.BlockSpec(memory_space=pltpu.SMEM) if i < smem else vmem for i in range(len(operands))
    ]
    size = sum(math.prod(o.shape) * o.dtype.itemsize for o in operands)
    return pl.pallas_call(
        lambda *refs: kernel(plan, *refs),
        out_shape=[jax.ShapeDtypeStruct(s, d) for s, d in outs],
        in_specs=in_specs,
        out_specs=[vmem] * len(outs),
        scratch_shapes=[pltpu.VMEM(s, d) for s, d in scratch],
        cost_estimate=pl.CostEstimate(flops=flops, bytes_accessed=size, transcendentals=0),
        name=kernel.__name__,
    )(*operands)


def swept(plan, neutral, tube_state, end_coupling, block_inverse):
    highest = lax.Precision.HIGHEST
    count = lax.axis_size("lev")
    wind = neutral.reshape(plan.tubes, plan.fields, plan.points).transpose(1, 0, 2)

    def solve(vector):
        return jnp.einsum("fpq,ftq->ftp", block_inverse, vector, precision=highest)

    forcing = tube_state + wind
    state = solve(forcing)
    for _ in range(SWEEPS):
        from_left = lax.ppermute(state[:, :, -1], "lev", [(i, i + 1) for i in range(count - 1)])
        from_right = lax.ppermute(state[:, :, 0], "lev", [(i + 1, i) for i in range(count - 1)])
        coupled = forcing.at[:, :, 0].add(end_coupling * from_left)
        coupled = coupled.at[:, :, -1].add(end_coupling * from_right)
        state = solve(coupled)
    return state, wind


def on_device(
    spectral,
    synthesis,
    analysis,
    interp_weights,
    tube_source,
    tube_column,
    weight_ids,
    tube_state,
    collision,
    end_coupling,
    block_inverse,
):
    sources = lax.axis_size(("grp", "band"))
    plan = Plan(
        sources, spectral.shape, synthesis.shape, interp_weights.shape, tube_state.shape
    )
    me = lax.axis_index(("grp", "band")).astype(I32).reshape(1)
    by_owner = (sources, plan.tubes)
    forward_table, backward_table = fourier_tables(plan)

    (sent,) = call(
        plan, synthesis_kernel, [((plan.rows, plan.columns), BF)], (spectral, synthesis)
    )
    fourier = exchange(plan, sent)
    weights, pick, pick_t, seat, seat_t = call(
        plan,
        routing_kernel,
        [
            ((plan.matrices * plan.points, plan.block), BF),
            ((plan.slots, plan.table), BF),
            ((plan.table, plan.slots), BF),
            ((plan.tubes, plan.slots), BF),
            ((plan.slots, plan.tubes), BF),
        ],
        (
            me,
            tube_source.reshape(by_owner),
            tube_column.reshape(by_owner),
            weight_ids.reshape(by_owner),
            interp_weights,
        ),
        smem=1,
        flops=1 << 31,
    )
    (sent,) = call(
        plan,
        neutral_kernel,
        [((plan.slots, plan.values), BF)],
        (fourier, forward_table, weights, pick),
        scratch=[
            ((plan.fields * plan.cells, plan.block), BF),
            ((plan.table, plan.values), BF),
        ],
    )
    arrived = exchange(plan, sent)
    if lax.axis_size("lev") == 1:
        state, sent = call(
            plan,
            tube_kernel,
            [(tube_state.shape, F32), ((plan.slots, plan.values), BF)],
            (arrived, seat, seat_t, tube_state, collision, block_inverse),
            scratch=[((plan.tubes, plan.values), BF)],
        )
    else:
        neutral = dot(seat, arrived)
        state, wind = swept(plan, neutral, tube_state, end_coupling, block_inverse)
        drag = (collision[None, :, :] * (state - wind)).astype(BF)
        drag = drag.transpose(1, 0, 2).reshape(plan.tubes, plan.values)
        sent = dot(seat_t, drag).astype(BF)
    contrib = exchange(plan, sent)
    (sent,) = call(
        plan,
        tendency_kernel,
        [((plan.rows, plan.columns), BF)],
        (contrib, backward_table, weights, pick_t),
        scratch=[
            ((plan.fields * plan.cells, plan.matrices * plan.points), BF),
            ((plan.width * plan.lon_pad, plan.lat_local * plan.half), F32),
        ],
    )
    analysed = exchange(plan, sent)
    (spectral_new,) = call(
        plan, analysis_kernel, [(spectral.shape, F32)], (analysed, analysis, spectral)
    )
    return spectral_new, state


def solution(mesh):
    placed = (
        P(("grp", "band"), None, "lev"),
        P(("grp", "band"), None, None),
        P(("grp", "band"), None, None),
        P(),
        P(),
        P(),
        P(),
        P(None, ("grp", "band"), "lev"),
        P(("grp", "band"), "lev"),
        P(None, ("grp", "band")),
        P(None, "lev", None),
    )
    return jax.shard_map(
        on_device,
        mesh=mesh,
        in_specs=placed,
        out_specs=(P(("grp", "band"), None, "lev"), P(None, ("grp", "band"), "lev")),
        check_vma=False,
    )
```

```python
import math

import jax
import jax.numpy as jnp
import numpy as np
from jax import lax
from jax.experimental import pallas as pl
from jax.experimental.pallas import tpu as pltpu
from jax.sharding import Mesh
from jax.sharding import PartitionSpec as P

LON = 192
SWEEPS = 4
BF = jnp.bfloat16
F32 = jnp.float32
I32 = jnp.int32
ALL = ("grp", "hold", "rest")
GROUP = ("grp", "rest")
VMEM_LIMIT = 24 << 20


def dot(a, b):
    return jnp.dot(a, b, preferred_element_type=F32)


def dot_nt(a, b):
    return lax.dot_general(a, b, (((1,), (1,)), ((), ())), preferred_element_type=F32)


def dot_tn(a, b):
    return lax.dot_general(a, b, (((0,), (0,)), ((), ())), preferred_element_type=F32)


def split(x):
    high = x.astype(BF)
    return high, (x - high.astype(F32)).astype(BF)


def iota(shape, dim):
    return lax.broadcasted_iota(I32, shape, dim)


def onehot(mask):
    return mask.astype(F32).astype(BF)


class Plan:
    def __init__(self, grp, copies, rest, spectral, synthesis, weights, tube_state):
        self.grp, self.copies, self.rest = grp, copies, rest
        self.sources = grp * copies * rest
        self.members = grp * rest
        self.wave_local, self.latitudes, self.degrees = synthesis
        self.waves = self.wave_local * self.sources
        self.lat_local = self.latitudes // self.sources
        self.lat_held = self.lat_local * copies
        self.columns = spectral[2]
        self.fields, self.tubes, self.points = tube_state
        self.matrices, _, self.block = weights
        self.levels = self.columns // (2 * self.fields)
        self.width = self.block // self.levels
        self.lon_blocks = LON // self.width
        self.lon_pad = -(-self.lon_blocks // 16) * 16
        self.capacity = 2 * self.tubes // self.sources
        self.slots = self.sources * self.capacity
        self.slots_held = self.members * self.capacity
        self.rows = self.wave_local * self.latitudes
        self.rows_sent = self.rows * copies
        self.cells = self.lat_local * self.lon_pad
        self.table = self.matrices * self.cells
        self.values = self.fields * self.points
        self.half = self.fields * self.levels


def chosen_rows(origin, count):
    origin = np.asarray(origin).reshape(-1)
    return jnp.asarray((origin[:, None] == np.arange(count)[None, :]).astype(BF))


def column_order(plan):
    natural = np.arange(plan.columns).reshape(plan.levels, plan.fields, 2)
    return chosen_rows(natural.transpose(2, 1, 0), plan.columns).T


def block_order(plan):
    natural = np.arange(plan.block).reshape(plan.levels, plan.width)
    return chosen_rows(natural.T, plan.block).T


def wave_rows(plan):
    p = plan
    index = np.arange(p.rows).reshape(p.wave_local, p.grp, p.copies, p.rest, p.lat_local)
    index = index.transpose(1, 3, 2, 0, 4)[:, None]
    return np.broadcast_to(
        index, (p.grp, p.copies, p.rest, p.copies, p.wave_local, p.lat_local)
    )


def latitude_rows(plan):
    p = plan
    index = np.arange(p.rows_sent).reshape(p.sources, p.copies, p.wave_local, p.lat_local)
    return index.transpose(1, 3, 0, 2)


def inverse_rows(plan):
    p = plan
    index = np.arange(p.rows_sent).reshape(p.copies, p.lat_local, p.sources, p.wave_local)
    return index.transpose(2, 0, 3, 1)


def joined_rows(plan):
    origin = np.ascontiguousarray(wave_rows(plan)).reshape(-1)
    return jnp.asarray((np.arange(plan.rows)[:, None] == origin[None, :]).astype(BF))


def fourier_tables(plan):
    wave = np.arange(plan.waves)
    lon = np.arange(LON)
    angle = 2.0 * math.pi * ((wave[:, None] * lon[None, :]) % LON) / LON
    full = np.stack([np.cos(angle), -np.sin(angle)], 0)
    full = full.reshape(2, plan.waves, plan.lon_blocks, plan.width)
    full = np.pad(full, ((0, 0), (0, 0), (0, plan.lon_pad - plan.lon_blocks), (0, 0)))
    forward = full.transpose(3, 2, 0, 1).reshape(plan.width * plan.lon_pad, 2 * plan.waves)
    high = forward.astype(BF)
    low = (forward - high.astype(np.float64)).astype(BF)
    synthesis = np.concatenate([high, low], 1)
    analysis = np.concatenate([high.T, low.T, high.T], 1)
    return jnp.asarray(synthesis), jnp.asarray(analysis)


def exchange(array, axes, count):
    shaped = array.reshape(count, array.shape[0] // count, array.shape[1])
    moved = lax.all_to_all(shaped, axes, split_axis=0, concat_axis=0, tiled=True)
    return moved.reshape(array.shape)


def synthesis_kernel(plan, spectral, synthesis_t, order, rows, out):
    parts = []
    for wave in range(plan.wave_local):
        moved = dot(spectral[wave], order[...]).astype(BF)
        parts.append(dot_tn(synthesis_t[wave], moved).astype(BF))
    out[...] = dot(rows[...], jnp.concatenate(parts, 0)).astype(BF)


def routing_kernel(
    plan, me, owners, columns, weight_of, weights, reorder, weights_out, pick, pick_t, seat, seat_t
):
    p = plan
    mine_g, mine_h, mine_l = me[0], me[1], me[2]
    tubes, capacity = p.tubes, p.capacity
    halves = owners.shape[0] // p.sources
    lanes = owners.shape[1]
    for matrix in range(p.matrices):
        rows = slice(matrix * p.points, (matrix + 1) * p.points)
        weights_out[rows, :] = dot(weights[matrix], reorder[...]).astype(BF)

    column = columns[...]
    cell = column
    for step in range(1, p.lat_local):
        late = (column >= step * p.lon_blocks).astype(I32)
        cell = cell + late * (p.lon_pad - p.lon_blocks)
    facts = [owners[...], cell + 1, weight_of[...]]
    facts = [fact.astype(F32).astype(BF) for fact in facts]

    def rows_of(fact, device):
        taken = []
        for half in range(halves):
            shape = (device.shape[0], p.sources * halves)
            taken.append(dot(onehot(device * halves + half == iota(shape, 1)), fact))
        return jnp.concatenate(taken, 1)

    member = iota((p.members, 1), 0)
    member_g, member_l = member // p.rest, member % p.rest
    device = (member_g * p.copies + mine_h) * p.rest + member_l
    owner, cell, matrix = [rows_of(fact, device) for fact in facts]
    before = onehot(iota((tubes, tubes), 0) < iota((tubes, tubes), 1))
    repeat = onehot(
        iota((p.slots_held, p.members), 0) // capacity == iota((p.slots_held, p.members), 1)
    )
    cell_all = dot(repeat, cell.astype(BF))
    matrix_all = dot(repeat, matrix.astype(BF))
    place = (iota((p.slots_held, tubes), 0) % capacity).astype(F32)
    ones = jnp.ones((16, tubes), BF)
    for copy in range(p.copies):
        source = ((mine_g * p.copies + copy) * p.rest + mine_l).astype(F32)
        mask = owner == source
        rank = jnp.where(mask, dot(onehot(mask), before), -1.0)
        chosen = dot(repeat, rank.astype(BF)) == place
        cell_slot = jnp.where(chosen, cell_all, 0.0)
        matrix_slot = jnp.where(chosen, matrix_all, 0.0)
        entry = jnp.sum(cell_slot + matrix_slot * p.cells, axis=1, keepdims=True)
        pick[copy] = onehot(entry.astype(I32) - 1 == iota((p.slots_held, p.table), 1))
        row = dot_nt(ones, cell_slot.astype(BF)) + dot_nt(ones, matrix_slot.astype(BF)) * p.cells
        row = row[0:1, :].astype(I32) - 1
        pick_t[copy] = onehot(row == iota((p.table, p.slots_held), 0))

    myself = jnp.zeros((16, 1), I32) + ((mine_g * p.copies + mine_h) * p.rest + mine_l)
    mine = rows_of(facts[0], myself)[0:1, :].astype(I32)
    square = (tubes, tubes)
    down, across = iota(square, 0), iota(square, 1)
    mine_col = jnp.sum(jnp.where(down == across, mine, 0), axis=1, keepdims=True)
    same = mine_col == mine
    rank_row = jnp.sum((same & (down < across)).astype(I32), axis=0, keepdims=True)
    rank_col = jnp.sum((same & (across < down)).astype(I32), axis=1, keepdims=True)

    def slot_of(source, rank):
        outer, inner = source // p.rest, source % p.rest
        g, h = outer // p.copies, outer % p.copies
        return ((g * p.rest + inner) * p.copies + h) * capacity + rank

    seat[...] = onehot(slot_of(mine_col, rank_col) == iota((tubes, p.slots), 1))
    seat_t[...] = onehot(slot_of(mine, rank_row) == iota((p.slots, tubes), 0))


def lane_masks(plan, rows):
    group = iota((rows, plan.half), 1) // plan.levels
    return [group == index for index in range(plan.fields)]


def chosen_lanes(plan, masks, pieces):
    result = pieces[0]
    for index in range(1, plan.fields):
        result = jnp.where(masks[index], pieces[index], result)
    return result


def rolled(plan, array, groups):
    groups = groups % plan.fields
    if groups == 0:
        return array
    return pltpu.roll(array, groups * plan.levels, axis=1)


def neutral_kernel(plan, arrived, rows, table, weights, pick, out, blocks, outcomes):
    p = plan
    by_lat = dot(rows[...], arrived[...]).astype(BF)
    stacks = []
    for lat in range(p.lat_held):
        part = by_lat[lat * p.waves : (lat + 1) * p.waves, :]
        stacks.append(jnp.concatenate([part[:, : p.half], part[:, p.half :]], 0))
    spectra = jnp.concatenate(stacks, 1)
    spectra = jnp.concatenate([spectra, spectra], 0)
    grid = dot(table[...], spectra) * p.waves ** (-0.5)
    masks = lane_masks(p, p.cells)
    per = p.fields
    for copy in range(p.copies):
        lats = range(copy * p.lat_local, (copy + 1) * p.lat_local)
        for step in range(p.width // per):
            pieces = []
            for index in range(per):
                start = (step * per + index) * p.lon_pad
                part = grid[start : start + p.lon_pad, :]
                pieces.append(
                    jnp.concatenate([part[:, lat * p.half : (lat + 1) * p.half] for lat in lats], 0)
                )
            for field in range(p.fields):
                turned = [rolled(p, pieces[index], index - field) for index in range(per)]
                first = (copy * p.fields + field) * p.cells
                blocks[first : first + p.cells, step * p.half : (step + 1) * p.half] = (
                    chosen_lanes(p, masks, turned).astype(BF)
                )
    values = blocks[...]
    for matrix in range(p.matrices):
        part = weights[matrix * p.points : (matrix + 1) * p.points, :]
        found = dot_nt(values, part).astype(BF)
        for copy in range(p.copies):
            for field in range(p.fields):
                first = (copy * p.fields + field) * p.cells
                outcomes[
                    copy,
                    matrix * p.cells : (matrix + 1) * p.cells,
                    field * p.points : (field + 1) * p.points,
                ] = found[first : first + p.cells, :]
    for copy in range(p.copies):
        taken = dot(pick[copy], outcomes[copy]).astype(BF)
        out[:, copy] = taken.reshape(p.members, p.capacity, p.values)


def tube_kernel(
    plan, arrived, seat, seat_t, tube_state, collision, inverse, state_out, out, drag
):
    neutral = dot(seat[...], arrived[...])
    for field in range(plan.fields):
        lanes = slice(field * plan.points, (field + 1) * plan.points)
        wind = neutral[:, lanes]
        force_high, force_low = split(tube_state[field] + wind)
        inverse_high, inverse_low = split(inverse[field])
        state = dot_nt(force_high, inverse_high) + (
            dot_nt(force_high, inverse_low) + dot_nt(force_low, inverse_high)
        )
        state_out[field] = state
        drag[:, lanes] = (collision[...] * (state - wind)).astype(BF)
    out[...] = dot(seat_t[...], drag[...]).astype(BF)


def tendency_kernel(plan, arrived, rows, table, weights, pick_t, out, sums, spread):
    p = plan
    for copy in range(p.copies):
        taken = arrived[:, copy].reshape(p.slots_held, p.values)
        found = dot(pick_t[copy], taken).astype(BF)
        for matrix in range(p.matrices):
            for field in range(p.fields):
                first = (copy * p.fields + field) * p.cells
                sums[
                    first : first + p.cells, matrix * p.points : (matrix + 1) * p.points
                ] = found[
                    matrix * p.cells : (matrix + 1) * p.cells,
                    field * p.points : (field + 1) * p.points,
                ]
    tendency = dot(sums[...], weights[...])
    masks = lane_masks(p, p.cells)
    per = p.fields
    for copy in range(p.copies):
        for step in range(p.width // per):
            pieces = []
            for field in range(p.fields):
                first = (copy * p.fields + field) * p.cells
                pieces.append(
                    tendency[first : first + p.cells, step * p.half : (step + 1) * p.half]
                )
            for index in range(per):
                turned = [rolled(p, pieces[field], field - index) for field in range(p.fields)]
                mixed = chosen_lanes(p, masks, turned)
                start = (step * per + index) * p.lon_pad
                for lat in range(p.lat_local):
                    held = copy * p.lat_local + lat
                    spread[
                        start : start + p.lon_pad, held * p.half : (held + 1) * p.half
                    ] = mixed[lat * p.lon_pad : (lat + 1) * p.lon_pad, :]
    high, low = split(spread[...])
    analysed = dot(table[...], jnp.concatenate([high, high, low], 0)) * LON ** (-0.5)
    analysed = analysed.astype(BF)
    stacks = []
    for lat in range(p.lat_held):
        lanes = analysed[:, lat * p.half : (lat + 1) * p.half]
        stacks.append(jnp.concatenate([lanes[: p.waves], lanes[p.waves :]], 1))
    out[...] = dot(rows[...], jnp.concatenate(stacks, 0)).astype(BF)


def analysis_kernel(plan, arrived, rows, order, analysis, spectral, out):
    joined = dot(rows[...], arrived[...]).astype(BF)
    natural = dot_nt(joined, order[...]).astype(BF)
    for wave in range(plan.wave_local):
        part = natural[wave * plan.latitudes : (wave + 1) * plan.latitudes, :]
        out[wave] = spectral[wave].astype(F32) + dot(analysis[wave], part)


def call(plan, kernel, outs, operands, scratch=(), smem=0, flops=0):
    vmem = pl.BlockSpec(memory_space=pltpu.VMEM)
    in_specs = [
        pl.BlockSpec(memory_space=pltpu.SMEM) if i < smem else vmem for i in range(len(operands))
    ]
    size = sum(math.prod(o.shape) * o.dtype.itemsize for o in operands)
    return pl.pallas_call(
        lambda *refs: kernel(plan, *refs),
        out_shape=[jax.ShapeDtypeStruct(s, d) for s, d in outs],
        in_specs=in_specs,
        out_specs=[vmem] * len(outs),
        scratch_shapes=[pltpu.VMEM(s, d) for s, d in scratch],
        cost_estimate=pl.CostEstimate(flops=flops, bytes_accessed=size, transcendentals=0),
        compiler_params=pltpu.CompilerParams(vmem_limit_bytes=VMEM_LIMIT),
        name=kernel.__name__,
    )(*operands)


def swept(plan, neutral, tube_state, end_coupling, block_inverse):
    highest = lax.Precision.HIGHEST
    count = lax.axis_size("lev")
    wind = neutral.reshape(plan.tubes, plan.fields, plan.points).transpose(1, 0, 2)

    def solve(vector):
        return jnp.einsum("fpq,ftq->ftp", block_inverse, vector, precision=highest)

    forcing = tube_state + wind
    state = solve(forcing)
    for _ in range(SWEEPS):
        from_left = lax.ppermute(state[:, :, -1], "lev", [(i, i + 1) for i in range(count - 1)])
        from_right = lax.ppermute(state[:, :, 0], "lev", [(i + 1, i) for i in range(count - 1)])
        coupled = forcing.at[:, :, 0].add(end_coupling * from_left)
        coupled = coupled.at[:, :, -1].add(end_coupling * from_right)
        state = solve(coupled)
    return state, wind


def on_device(
    spectral,
    synthesis,
    analysis,
    interp_weights,
    tube_source,
    tube_column,
    weight_ids,
    tube_state,
    collision,
    end_coupling,
    block_inverse,
):
    plan = Plan(
        *[lax.axis_size(axis) for axis in ALL],
        spectral.shape,
        synthesis.shape,
        interp_weights.shape,
        tube_state.shape,
    )
    p = plan
    me = jnp.stack([lax.axis_index(axis) for axis in ALL]).astype(I32)
    lanes = math.gcd(p.tubes, 128)
    by_lane = (p.sources * p.tubes // lanes, lanes)
    forward_table, backward_table = fourier_tables(p)
    order = column_order(p)

    (sent,) = call(
        p,
        synthesis_kernel,
        [((p.rows_sent, p.columns), BF)],
        (
            spectral,
            synthesis.transpose(0, 2, 1),
            order,
            chosen_rows(wave_rows(p), p.rows),
        ),
    )
    fourier = exchange(sent, ALL, p.sources)
    weights, pick, pick_t, seat, seat_t = call(
        p,
        routing_kernel,
        [
            ((p.matrices * p.points, p.block), BF),
            ((p.copies, p.slots_held, p.table), BF),
            ((p.copies, p.table, p.slots_held), BF),
            ((p.tubes, p.slots), BF),
            ((p.slots, p.tubes), BF),
        ],
        (
            me,
            tube_source.reshape(by_lane),
            tube_column.reshape(by_lane),
            weight_ids.reshape(by_lane),
            interp_weights,
            block_order(p),
        ),
        smem=1,
        flops=1 << 31,
    )
    by_slot = (p.members, p.copies, p.capacity, p.values)
    flat = (p.slots, p.values)
    (sent,) = call(
        p,
        neutral_kernel,
        [(by_slot, BF)],
        (fourier, chosen_rows(latitude_rows(p), p.rows_sent), forward_table, weights, pick),
        scratch=[
            ((p.copies * p.fields * p.cells, p.block), BF),
            ((p.copies, p.table, p.values), BF),
        ],
    )
    arrived = exchange(sent.reshape(flat), GROUP, p.members)
    if lax.axis_size("lev") == 1:
        state, sent = call(
            p,
            tube_kernel,
            [(tube_state.shape, F32), (flat, BF)],
            (arrived, seat, seat_t, tube_state, collision, block_inverse),
            scratch=[((p.tubes, p.values), BF)],
        )
    else:
        state, wind = swept(p, dot(seat, arrived), tube_state, end_coupling, block_inverse)
        drag = (collision[None, :, :] * (state - wind)).astype(BF)
        drag = drag.transpose(1, 0, 2).reshape(p.tubes, p.values)
        sent = dot(seat_t, drag).astype(BF)
    contrib = exchange(sent, GROUP, p.members)
    (sent,) = call(
        p,
        tendency_kernel,
        [((p.rows_sent, p.columns), BF)],
        (
            contrib.reshape(by_slot),
            chosen_rows(inverse_rows(p), p.rows_sent),
            backward_table,
            weights,
            pick_t,
        ),
        scratch=[
            ((p.copies * p.fields * p.cells, p.matrices * p.points), BF),
            ((p.width * p.lon_pad, p.lat_held * p.half), F32),
        ],
    )
    analysed = exchange(sent, ALL, p.sources)
    (spectral_new,) = call(
        p,
        analysis_kernel,
        [(spectral.shape, F32)],
        (analysed, joined_rows(p), order, analysis, spectral),
    )
    return spectral_new, state


def solution(mesh):
    grp, band, lev = (mesh.shape[axis] for axis in ("grp", "band", "lev"))
    copies = 2 if band % 2 == 0 else 1
    parts = mesh.devices.reshape(grp, copies, band // copies, lev)
    mesh = Mesh(parts, ("grp", "hold", "rest", "lev"))
    placed = (
        P(ALL, None, "lev"),
        P(ALL, None, None),
        P(ALL, None, None),
        P(),
        P(),
        P(),
        P(),
        P(None, ALL, "lev"),
        P(ALL, "lev"),
        P(None, ALL),
        P(None, "lev", None),
    )
    return jax.shard_map(
        on_device,
        mesh=mesh,
        in_specs=placed,
        out_specs=(P(ALL, None, "lev"), P(None, ALL, "lev")),
        check_vma=False,
    )
```

```python
import math

import jax
import jax.numpy as jnp
import numpy as np
from jax import lax
from jax.experimental import pallas as pl
from jax.experimental.pallas import tpu as pltpu
from jax.sharding import Mesh
from jax.sharding import PartitionSpec as P

LON = 192
SWEEPS = 4
BF = jnp.bfloat16
F32 = jnp.float32
I32 = jnp.int32
ALL = ("grp", "hold", "rest")
GROUP = ("grp", "rest")
VMEM_LIMIT = 24 << 20


def dot(a, b):
    return jnp.dot(a, b, preferred_element_type=F32)


def dot_nt(a, b):
    return lax.dot_general(a, b, (((1,), (1,)), ((), ())), preferred_element_type=F32)


def dot_tn(a, b):
    return lax.dot_general(a, b, (((0,), (0,)), ((), ())), preferred_element_type=F32)


def split(x):
    high = x.astype(BF)
    return high, (x - high.astype(F32)).astype(BF)


def iota(shape, dim):
    return lax.broadcasted_iota(I32, shape, dim)


def onehot(mask):
    return mask.astype(F32).astype(BF)


class Plan:
    def __init__(self, grp, copies, rest, spectral, synthesis, weights, tube_state):
        self.grp, self.copies, self.rest = grp, copies, rest
        self.sources = grp * copies * rest
        self.members = grp * rest
        self.wave_local, self.latitudes, self.degrees = synthesis
        self.waves = self.wave_local * self.sources
        self.lat_local = self.latitudes // self.sources
        self.lat_held = self.lat_local * copies
        self.columns = spectral[2]
        self.fields, self.tubes, self.points = tube_state
        self.matrices, _, self.block = weights
        self.levels = self.columns // (2 * self.fields)
        self.width = self.block // self.levels
        self.lon_blocks = LON // self.width
        self.lon_pad = -(-self.lon_blocks // 16) * 16
        self.capacity = 2 * self.tubes // self.sources
        self.slots = self.sources * self.capacity
        self.slots_held = self.members * self.capacity
        self.rows = self.wave_local * self.latitudes
        self.rows_sent = self.rows * copies
        self.cells = self.lat_local * self.lon_pad
        self.table = self.matrices * self.cells
        self.values = self.fields * self.points
        self.half = self.fields * self.levels


def chosen_rows(origin, count):
    origin = np.asarray(origin).reshape(-1)
    return jnp.asarray((origin[:, None] == np.arange(count)[None, :]).astype(BF))


def column_order(plan):
    natural = np.arange(plan.columns).reshape(plan.levels, plan.fields, 2)
    return chosen_rows(natural.transpose(2, 1, 0), plan.columns).T


def block_order(plan):
    natural = np.arange(plan.block).reshape(plan.levels, plan.width)
    return chosen_rows(natural.T, plan.block).T


def wave_rows(plan):
    p = plan
    index = np.arange(p.rows).reshape(p.wave_local, p.grp, p.copies, p.rest, p.lat_local)
    return index.transpose(1, 3, 2, 0, 4)


def latitude_rows(plan):
    p = plan
    index = np.arange(p.rows_sent).reshape(p.sources, p.copies, p.wave_local, p.lat_local)
    return index.transpose(1, 3, 0, 2)


def inverse_rows(plan):
    p = plan
    index = np.arange(p.rows_sent).reshape(p.copies, p.lat_local, p.sources, p.wave_local)
    return index.transpose(2, 0, 3, 1)


def fourier_tables(plan):
    wave = np.arange(plan.waves)
    lon = np.arange(LON)
    angle = 2.0 * math.pi * ((wave[:, None] * lon[None, :]) % LON) / LON
    full = np.stack([np.cos(angle), -np.sin(angle)], 0)
    full = full.reshape(2, plan.waves, plan.lon_blocks, plan.width)
    full = np.pad(full, ((0, 0), (0, 0), (0, plan.lon_pad - plan.lon_blocks), (0, 0)))
    forward = full.transpose(3, 2, 0, 1).reshape(plan.width * plan.lon_pad, 2 * plan.waves)
    high = forward.astype(BF)
    low = (forward - high.astype(np.float64)).astype(BF)
    synthesis = np.concatenate([high, low], 1)
    analysis = np.concatenate([high.T, low.T, high.T], 1)
    return jnp.asarray(synthesis), jnp.asarray(analysis)


def exchange(array, axes, count):
    shaped = array.reshape(count, array.shape[0] // count, array.shape[1])
    moved = lax.all_to_all(shaped, axes, split_axis=0, concat_axis=0, tiled=True)
    return moved.reshape(array.shape)


def synthesis_kernel(plan, wait, spectral, synthesis_t, order, rows, out):
    p = plan
    total = 0.0
    for wave in range(p.wave_local):
        moved = dot(spectral[wave], order[...]).astype(BF)
        here = rows[:, wave * p.latitudes : (wave + 1) * p.latitudes]
        placed = dot_nt(here, synthesis_t[wave]).astype(BF)
        total = total + dot(placed, moved)
    moved = total.astype(BF).reshape(p.grp, p.rows // p.grp, p.columns)
    for copy in range(p.copies):
        out[:, copy] = moved


def routing_kernel(
    plan,
    wait,
    me,
    owners,
    columns,
    weight_of,
    weights,
    reorder,
    weights_out,
    pick_t,
    seat_t,
):
    p = plan
    mine_g, mine_h, mine_l = me[0], me[1], me[2]
    tubes, capacity = p.tubes, p.capacity
    halves = owners.shape[0] // p.sources
    lanes = owners.shape[1]
    column = columns[...]
    cell = column
    for step in range(1, p.lat_local):
        late = (column >= step * p.lon_blocks).astype(I32)
        cell = cell + late * (p.lon_pad - p.lon_blocks)
    facts = [owners[...], cell + 1, weight_of[...]]
    facts = [fact.astype(F32).astype(BF) for fact in facts]

    def rows_of(fact, device):
        taken = []
        for half in range(halves):
            shape = (device.shape[0], p.sources * halves)
            taken.append(dot(onehot(device * halves + half == iota(shape, 1)), fact))
        return jnp.concatenate(taken, 1)

    member = iota((p.members, 1), 0)
    member_g, member_l = member // p.rest, member % p.rest
    device = (member_g * p.copies + mine_h) * p.rest + member_l
    owner, cell, matrix = [rows_of(fact, device) for fact in facts]
    before = onehot(iota((tubes, tubes), 0) < iota((tubes, tubes), 1))
    repeat = onehot(
        iota((p.slots_held, p.members), 0) // capacity == iota((p.slots_held, p.members), 1)
    )
    cell_all = dot(repeat, cell.astype(BF))
    matrix_all = dot(repeat, matrix.astype(BF))
    place = (iota((p.slots_held, tubes), 0) % capacity).astype(F32)
    ones = jnp.ones((16, tubes), BF)
    for copy in range(p.copies):
        source = ((mine_g * p.copies + copy) * p.rest + mine_l).astype(F32)
        mask = owner == source
        rank = jnp.where(mask, dot(onehot(mask), before), -1.0)
        chosen = dot(repeat, rank.astype(BF)) == place
        cell_slot = jnp.where(chosen, cell_all, 0.0)
        matrix_slot = jnp.where(chosen, matrix_all, 0.0)
        row = dot_nt(ones, cell_slot.astype(BF)) + dot_nt(ones, matrix_slot.astype(BF)) * p.cells
        row = row[0:1, :].astype(I32) - 1
        pick_t[copy] = onehot(row == iota((p.table, p.slots_held), 0))

    myself = jnp.zeros((16, 1), I32) + ((mine_g * p.copies + mine_h) * p.rest + mine_l)
    mine = rows_of(facts[0], myself)[0:1, :].astype(I32)
    square = (tubes, tubes)
    down, across = iota(square, 0), iota(square, 1)
    mine_col = jnp.sum(jnp.where(down == across, mine, 0), axis=1, keepdims=True)
    same = mine_col == mine
    rank_row = jnp.sum((same & (down < across)).astype(I32), axis=0, keepdims=True)

    def slot_of(source, rank):
        outer, inner = source // p.rest, source % p.rest
        g, h = outer // p.copies, outer % p.copies
        return ((g * p.rest + inner) * p.copies + h) * capacity + rank

    seat_t[...] = onehot(slot_of(mine, rank_row) == iota((p.slots, tubes), 0))

    wait(5)
    wait(4)
    for matrix in range(p.matrices):
        rows = slice(matrix * p.points, (matrix + 1) * p.points)
        weights_out[rows, :] = dot(weights[matrix], reorder[...]).astype(BF)


def lane_masks(plan, rows):
    group = iota((rows, plan.half), 1) // plan.levels
    return [group == index for index in range(plan.fields)]


def chosen_lanes(plan, masks, pieces):
    result = pieces[0]
    for index in range(1, plan.fields):
        result = jnp.where(masks[index], pieces[index], result)
    return result


def rolled(plan, array, groups):
    groups = groups % plan.fields
    if groups == 0:
        return array
    return pltpu.roll(array, groups * plan.levels, axis=1)


def neutral_kernel(plan, wait, arrived, rows, table, weights, pick_t, out, blocks, outcomes):
    p = plan
    by_lat = dot(rows[...], arrived[...]).astype(BF)
    stacks = []
    for lat in range(p.lat_held):
        part = by_lat[lat * p.waves : (lat + 1) * p.waves, :]
        stacks.append(jnp.concatenate([part[:, : p.half], part[:, p.half :]], 0))
    spectra = jnp.concatenate(stacks, 1)
    spectra = jnp.concatenate([spectra, spectra], 0)
    grid = dot(table[...], spectra) * p.waves ** (-0.5)
    masks = lane_masks(p, p.cells)
    per = p.fields
    for copy in range(p.copies):
        lats = range(copy * p.lat_local, (copy + 1) * p.lat_local)
        for step in range(p.width // per):
            pieces = []
            for index in range(per):
                start = (step * per + index) * p.lon_pad
                part = grid[start : start + p.lon_pad, :]
                pieces.append(
                    jnp.concatenate([part[:, lat * p.half : (lat + 1) * p.half] for lat in lats], 0)
                )
            for field in range(p.fields):
                turned = [rolled(p, pieces[index], index - field) for index in range(per)]
                first = (copy * p.fields + field) * p.cells
                blocks[first : first + p.cells, step * p.half : (step + 1) * p.half] = (
                    chosen_lanes(p, masks, turned).astype(BF)
                )
    values = blocks[...]
    for matrix in range(p.matrices):
        part = weights[matrix * p.points : (matrix + 1) * p.points, :]
        found = dot_nt(values, part).astype(BF)
        for copy in range(p.copies):
            for field in range(p.fields):
                first = (copy * p.fields + field) * p.cells
                outcomes[
                    copy,
                    matrix * p.cells : (matrix + 1) * p.cells,
                    field * p.points : (field + 1) * p.points,
                ] = found[first : first + p.cells, :]
    for copy in range(p.copies):
        taken = dot_tn(pick_t[copy], outcomes[copy]).astype(BF)
        out[:, copy] = taken.reshape(p.members, p.capacity, p.values)


def tube_kernel(
    plan, wait, arrived, seat_t, tube_state, collision, inverse, state_out, out, drag, held, done
):
    neutral = dot_tn(seat_t[...], arrived[...])
    copies = []
    for field in range(plan.fields):
        lanes = slice(field * plan.points, (field + 1) * plan.points)
        wind = neutral[:, lanes]
        force_high, force_low = split(tube_state[field] + wind)
        inverse_high, inverse_low = split(inverse[field])
        state = dot_nt(force_high, inverse_high) + (
            dot_nt(force_high, inverse_low) + dot_nt(force_low, inverse_high)
        )
        held[field] = state
        copies.append(
            pltpu.make_async_copy(held.at[field], state_out.at[field], done.at[field])
        )
        copies[-1].start()
        drag[:, lanes] = (collision[...] * (state - wind)).astype(BF)
    out[...] = dot(seat_t[...], drag[...]).astype(BF)
    for copy in copies:
        copy.wait()


def tendency_kernel(plan, wait, arrived, rows, table, weights, pick_t, out, sums, spread):
    p = plan
    for copy in range(p.copies):
        taken = arrived[:, copy].reshape(p.slots_held, p.values)
        found = dot(pick_t[copy], taken).astype(BF)
        for matrix in range(p.matrices):
            for field in range(p.fields):
                first = (copy * p.fields + field) * p.cells
                sums[
                    first : first + p.cells, matrix * p.points : (matrix + 1) * p.points
                ] = found[
                    matrix * p.cells : (matrix + 1) * p.cells,
                    field * p.points : (field + 1) * p.points,
                ]
    tendency = dot(sums[...], weights[...])
    masks = lane_masks(p, p.cells)
    per = p.fields
    for copy in range(p.copies):
        for step in range(p.width // per):
            pieces = []
            for field in range(p.fields):
                first = (copy * p.fields + field) * p.cells
                pieces.append(
                    tendency[first : first + p.cells, step * p.half : (step + 1) * p.half]
                )
            for index in range(per):
                turned = [rolled(p, pieces[field], field - index) for field in range(p.fields)]
                mixed = chosen_lanes(p, masks, turned)
                start = (step * per + index) * p.lon_pad
                for lat in range(p.lat_local):
                    held = copy * p.lat_local + lat
                    spread[
                        start : start + p.lon_pad, held * p.half : (held + 1) * p.half
                    ] = mixed[lat * p.lon_pad : (lat + 1) * p.lon_pad, :]
    high, low = split(spread[...])
    analysed = dot(table[...], jnp.concatenate([high, high, low], 0)) * LON ** (-0.5)
    analysed = analysed.astype(BF)
    stacks = []
    for lat in range(p.lat_held):
        lanes = analysed[:, lat * p.half : (lat + 1) * p.half]
        stacks.append(jnp.concatenate([lanes[: p.waves], lanes[p.waves :]], 1))
    out[...] = dot(rows[...], jnp.concatenate(stacks, 0)).astype(BF)


def analysis_kernel(plan, wait, arrived, rows, order, analysis, spectral, out):
    joined = arrived[:, 0].astype(F32)
    for copy in range(1, plan.copies):
        joined = joined + arrived[:, copy].astype(F32)
    joined = joined.reshape(plan.rows, plan.columns).astype(BF)
    natural = dot_tn(rows[...], joined).astype(BF)
    natural = dot_nt(natural, order[...]).astype(BF)
    for wave in range(plan.wave_local):
        part = natural[wave * plan.latitudes : (wave + 1) * plan.latitudes, :]
        out[wave] = spectral[wave].astype(F32) + dot(analysis[wave], part)


def call(
    plan, kernel, outs, operands, scratch=(), smem=0, fetched=(), late=(), stored=(), flops=0
):
    vmem = pl.BlockSpec(memory_space=pltpu.VMEM)
    hbm = pl.BlockSpec(memory_space=pltpu.HBM)
    scalar = pl.BlockSpec(memory_space=pltpu.SMEM)
    in_specs = [
        scalar if i < smem else hbm if i in fetched else vmem for i in range(len(operands))
    ]
    size = sum(math.prod(o.shape) * o.dtype.itemsize for o in operands)
    operands = [
        pltpu.with_memory_space_constraint(o, pltpu.HBM) if i in fetched else o
        for i, o in enumerate(operands)
    ]
    held = [pltpu.VMEM(s, d) for s, d in scratch]
    for i in stored:
        held += [pltpu.VMEM(*outs[i]), pltpu.SemaphoreType.DMA(outs[i][0][:1])]
    if fetched:
        held += [pltpu.VMEM(operands[i].shape, operands[i].dtype) for i in fetched]
        held += [pltpu.SemaphoreType.DMA((len(fetched),))]

    def body(*refs):
        refs = list(refs)
        copies = {}
        for place, i in enumerate(fetched):
            target = refs[place - 1 - len(fetched)]
            copies[i] = pltpu.make_async_copy(refs[i], target, refs[-1].at[place])
            copies[i].start()
        for place, i in enumerate(fetched):
            refs[i] = refs[place - 1 - len(fetched)]
        for i in fetched:
            if i not in late:
                copies[i].wait()
        if fetched:
            refs = refs[: -1 - len(fetched)]
        kernel(plan, lambda i: copies[i].wait(), *refs)

    return pl.pallas_call(
        body,
        out_shape=[jax.ShapeDtypeStruct(s, d) for s, d in outs],
        in_specs=in_specs,
        out_specs=[hbm if i in stored else vmem for i in range(len(outs))],
        scratch_shapes=held,
        cost_estimate=pl.CostEstimate(flops=flops, bytes_accessed=size, transcendentals=0),
        compiler_params=pltpu.CompilerParams(vmem_limit_bytes=VMEM_LIMIT),
        name=kernel.__name__,
    )(*operands)


def swept(plan, neutral, tube_state, end_coupling, block_inverse):
    highest = lax.Precision.HIGHEST
    count = lax.axis_size("lev")
    wind = neutral.reshape(plan.tubes, plan.fields, plan.points).transpose(1, 0, 2)

    def solve(vector):
        return jnp.einsum("fpq,ftq->ftp", block_inverse, vector, precision=highest)

    forcing = tube_state + wind
    state = solve(forcing)
    for _ in range(SWEEPS):
        from_left = lax.ppermute(state[:, :, -1], "lev", [(i, i + 1) for i in range(count - 1)])
        from_right = lax.ppermute(state[:, :, 0], "lev", [(i + 1, i) for i in range(count - 1)])
        coupled = forcing.at[:, :, 0].add(end_coupling * from_left)
        coupled = coupled.at[:, :, -1].add(end_coupling * from_right)
        state = solve(coupled)
    return state, wind


def on_device(
    spectral,
    synthesis,
    analysis,
    interp_weights,
    tube_source,
    tube_column,
    weight_ids,
    tube_state,
    collision,
    end_coupling,
    block_inverse,
):
    plan = Plan(
        *[lax.axis_size(axis) for axis in ALL],
        spectral.shape,
        synthesis.shape,
        interp_weights.shape,
        tube_state.shape,
    )
    p = plan
    me = jnp.stack([lax.axis_index(axis) for axis in ALL]).astype(I32)
    lanes = math.gcd(p.tubes, 128)
    by_lane = (p.sources * p.tubes // lanes, lanes)
    forward_table, backward_table = fourier_tables(p)
    order = column_order(p)
    wave_order = chosen_rows(wave_rows(p), p.rows)

    (sent,) = call(
        p,
        synthesis_kernel,
        [((p.grp, p.copies, p.rows // p.grp, p.columns), BF)],
        (spectral, synthesis.transpose(0, 2, 1), order, wave_order),
        fetched=(0, 1, 2, 3),
    )
    flat = (p.rows_sent, p.columns)
    fourier = exchange(sent.reshape(flat), ALL, p.sources)
    weights, pick_t, seat_t = call(
        p,
        routing_kernel,
        [
            ((p.matrices * p.points, p.block), BF),
            ((p.copies, p.table, p.slots_held), BF),
            ((p.slots, p.tubes), BF),
        ],
        (
            me,
            tube_source.reshape(by_lane),
            tube_column.reshape(by_lane),
            weight_ids.reshape(by_lane),
            interp_weights,
            block_order(p),
        ),
        smem=1,
        fetched=(1, 2, 3, 5, 4),
        late=(4, 5),
        flops=1 << 31,
    )
    by_slot = (p.members, p.copies, p.capacity, p.values)
    flat = (p.slots, p.values)
    (sent,) = call(
        p,
        neutral_kernel,
        [(by_slot, BF)],
        (fourier, chosen_rows(latitude_rows(p), p.rows_sent), forward_table, weights, pick_t),
        scratch=[
            ((p.copies * p.fields * p.cells, p.block), BF),
            ((p.copies, p.table, p.values), BF),
        ],
    )
    arrived = exchange(sent.reshape(flat), GROUP, p.members)
    if lax.axis_size("lev") == 1:
        state, sent = call(
            p,
            tube_kernel,
            [(tube_state.shape, F32), (flat, BF)],
            (arrived, seat_t, tube_state, collision, block_inverse),
            scratch=[((p.tubes, p.values), BF)],
            stored=(0,),
        )
    else:
        state, wind = swept(p, dot_tn(seat_t, arrived), tube_state, end_coupling, block_inverse)
        drag = (collision[None, :, :] * (state - wind)).astype(BF)
        drag = drag.transpose(1, 0, 2).reshape(p.tubes, p.values)
        sent = dot(seat_t, drag).astype(BF)
    contrib = exchange(sent, GROUP, p.members)
    (sent,) = call(
        p,
        tendency_kernel,
        [((p.rows_sent, p.columns), BF)],
        (
            contrib.reshape(by_slot),
            chosen_rows(inverse_rows(p), p.rows_sent),
            backward_table,
            weights,
            pick_t,
        ),
        scratch=[
            ((p.copies * p.fields * p.cells, p.matrices * p.points), BF),
            ((p.width * p.lon_pad, p.lat_held * p.half), F32),
        ],
    )
    analysed = exchange(sent, ALL, p.sources)
    (spectral_new,) = call(
        p,
        analysis_kernel,
        [(spectral.shape, F32)],
        (
            analysed.reshape(p.grp, p.copies, p.rows // p.grp, p.columns),
            wave_order,
            order,
            analysis,
            spectral,
        ),
    )
    return spectral_new, state


def solution(mesh):
    grp, band, lev = (mesh.shape[axis] for axis in ("grp", "band", "lev"))
    copies = 2 if band % 2 == 0 else 1
    parts = mesh.devices.reshape(grp, copies, band // copies, lev)
    mesh = Mesh(parts, ("grp", "hold", "rest", "lev"))
    placed = (
        P(ALL, None, "lev"),
        P(ALL, None, None),
        P(ALL, None, None),
        P(),
        P(),
        P(),
        P(),
        P(None, ALL, "lev"),
        P(ALL, "lev"),
        P(None, ALL),
        P(None, "lev", None),
    )
    return jax.shard_map(
        on_device,
        mesh=mesh,
        in_specs=placed,
        out_specs=(P(ALL, None, "lev"), P(None, ALL, "lev")),
        check_vma=False,
    )
```

```python
import math

import jax
import jax.numpy as jnp
import numpy as np
from jax import lax
from jax.experimental import pallas as pl
from jax.experimental.pallas import tpu as pltpu
from jax.sharding import Mesh
from jax.sharding import PartitionSpec as P

LON = 192
SWEEPS = 4
BF = jnp.bfloat16
F32 = jnp.float32
I32 = jnp.int32
ALL = ("grp", "hold", "rest")
GROUP = ("grp", "rest")
VMEM_LIMIT = 24 << 20


def dot(a, b):
    return jnp.dot(a, b, preferred_element_type=F32)


def dot_nt(a, b):
    return lax.dot_general(a, b, (((1,), (1,)), ((), ())), preferred_element_type=F32)


def dot_tn(a, b):
    return lax.dot_general(a, b, (((0,), (0,)), ((), ())), preferred_element_type=F32)


def split(x):
    high = x.astype(BF)
    return high, (x - high.astype(F32)).astype(BF)


def iota(shape, dim):
    return lax.broadcasted_iota(I32, shape, dim)


def onehot(mask):
    return mask.astype(F32).astype(BF)


class Plan:
    def __init__(self, grp, copies, rest, spectral, synthesis, weights, tube_state):
        self.grp, self.copies, self.rest = grp, copies, rest
        self.sources = grp * copies * rest
        self.members = grp * rest
        self.wave_local, self.latitudes, self.degrees = synthesis
        self.waves = self.wave_local * self.sources
        self.lat_local = self.latitudes // self.sources
        self.lat_held = self.lat_local * copies
        self.columns = spectral[2]
        self.fields, self.tubes, self.points = tube_state
        self.matrices, _, self.block = weights
        self.levels = self.columns // (2 * self.fields)
        self.width = self.block // self.levels
        self.lon_blocks = LON // self.width
        fits = [
            n
            for n in range(1, self.lat_local + 1)
            if self.lat_local % n == 0 and n * self.lon_blocks % 8 == 0
        ]
        self.pack = fits[0] if fits else 1
        self.lon_pad = self.lon_blocks if fits else -(-self.lon_blocks // 8) * 8
        self.unit = self.pack * self.lon_pad
        self.capacity = 2 * self.tubes // self.sources
        self.slots = self.sources * self.capacity
        self.slots_held = self.members * self.capacity
        self.rows = self.wave_local * self.latitudes
        self.rows_sent = self.rows * copies
        self.cells = self.lat_local * self.lon_pad
        self.table = self.matrices * self.cells
        self.values = self.fields * self.points
        self.half = self.fields * self.levels


def chosen_rows(origin, count):
    origin = np.asarray(origin).reshape(-1)
    return jnp.asarray((origin[:, None] == np.arange(count)[None, :]).astype(BF))


def column_order(plan):
    natural = np.arange(plan.columns).reshape(plan.levels, plan.fields, 2)
    return chosen_rows(natural.transpose(2, 1, 0), plan.columns).T


def block_order(plan):
    natural = np.arange(plan.block).reshape(plan.levels, plan.width)
    return chosen_rows(natural.T, plan.block).T


def wave_rows(plan):
    p = plan
    index = np.arange(p.rows).reshape(p.wave_local, p.grp, p.copies, p.rest, p.lat_local)
    return index.transpose(1, 3, 2, 0, 4)


def strided_rows(plan, part, lat, wave):
    copy, local = lat // plan.lat_local, lat % plan.lat_local
    start = (copy * plan.wave_local + wave) * plan.lat_local + local + part * plan.rows_sent
    return pl.ds(start, plan.sources, stride=plan.copies * plan.wave_local * plan.lat_local)


def fourier_tables(plan):
    wave = np.arange(plan.waves).reshape(plan.sources, plan.wave_local).T.reshape(-1)
    lon = np.arange(LON)
    angle = 2.0 * math.pi * ((wave[:, None] * lon[None, :]) % LON) / LON
    full = np.stack([np.cos(angle), -np.sin(angle)], 0)
    full = full.reshape(2, plan.waves, plan.lon_blocks, plan.width)
    full = np.pad(full, ((0, 0), (0, 0), (0, plan.lon_pad - plan.lon_blocks), (0, 0)))
    forward = full.transpose(3, 2, 0, 1)[:, None]
    forward = np.broadcast_to(forward, (plan.width, plan.pack) + forward.shape[2:])
    forward = forward.reshape(plan.width * plan.unit, 2 * plan.waves)
    high = forward.astype(BF)
    low = (forward - high.astype(np.float64)).astype(BF)
    synthesis = np.concatenate([high, low], 1)
    analysis = np.concatenate([high.T, low.T, high.T], 1)
    return jnp.asarray(synthesis), jnp.asarray(analysis)


def exchange(array, axes, count):
    shaped = array.reshape(count, array.shape[0] // count, array.shape[1])
    moved = lax.all_to_all(shaped, axes, split_axis=0, concat_axis=0, tiled=True)
    return moved.reshape(array.shape)


def synthesis_kernel(plan, wait, spectral, synthesis_t, order, rows, out):
    p = plan
    total = 0.0
    for wave in range(p.wave_local):
        moved = dot(spectral[wave], order[...]).astype(BF)
        here = rows[:, wave * p.latitudes : (wave + 1) * p.latitudes]
        placed = dot_nt(here, synthesis_t[wave]).astype(BF)
        total = total + dot(placed, moved)
    moved = total.astype(BF).reshape(p.grp, p.rows // p.grp, p.columns)
    for copy in range(p.copies):
        out[:, copy] = moved


def routing_kernel(
    plan,
    wait,
    me,
    owners,
    columns,
    weight_of,
    weights,
    reorder,
    weights_out,
    pick_t,
    seat_t,
):
    p = plan
    mine_g, mine_h, mine_l = me[0], me[1], me[2]
    tubes, capacity = p.tubes, p.capacity
    halves = owners.shape[0] // p.sources
    lanes = owners.shape[1]
    column = columns[...]
    cell = column
    for step in range(1, p.lat_local):
        late = (column >= step * p.lon_blocks).astype(I32)
        cell = cell + late * (p.lon_pad - p.lon_blocks)
    facts = [owners[...], cell + 1, weight_of[...]]
    facts = [fact.astype(F32).astype(BF) for fact in facts]

    def rows_of(fact, device):
        taken = []
        for half in range(halves):
            shape = (device.shape[0], p.sources * halves)
            taken.append(dot(onehot(device * halves + half == iota(shape, 1)), fact))
        return jnp.concatenate(taken, 1)

    member = iota((p.members, 1), 0)
    member_g, member_l = member // p.rest, member % p.rest
    device = (member_g * p.copies + mine_h) * p.rest + member_l
    owner, cell, matrix = [rows_of(fact, device) for fact in facts]
    before = onehot(iota((tubes, tubes), 0) < iota((tubes, tubes), 1))
    repeat = onehot(
        iota((p.slots_held, p.members), 0) // capacity == iota((p.slots_held, p.members), 1)
    )
    cell_all = dot(repeat, cell.astype(BF))
    matrix_all = dot(repeat, matrix.astype(BF))
    place = (iota((p.slots_held, tubes), 0) % capacity).astype(F32)
    ones = jnp.ones((16, tubes), BF)
    for copy in range(p.copies):
        source = ((mine_g * p.copies + copy) * p.rest + mine_l).astype(F32)
        mask = owner == source
        rank = jnp.where(mask, dot(onehot(mask), before), -1.0)
        taken = dot(repeat, rank.astype(BF)) == place
        cell_slot = jnp.where(taken, cell_all, 0.0)
        matrix_slot = jnp.where(taken, matrix_all, 0.0)
        row = dot_nt(ones, cell_slot.astype(BF)) + dot_nt(ones, matrix_slot.astype(BF)) * p.cells
        row = row[0:1, :].astype(I32) - 1
        pick_t[copy] = onehot(row == iota((p.table, p.slots_held), 0))

    myself = jnp.zeros((16, 1), I32) + ((mine_g * p.copies + mine_h) * p.rest + mine_l)
    mine = rows_of(facts[0], myself)[0:1, :].astype(I32)
    square = (tubes, tubes)
    down, across = iota(square, 0), iota(square, 1)
    mine_col = jnp.sum(jnp.where(down == across, mine, 0), axis=1, keepdims=True)
    same = mine_col == mine
    rank_row = jnp.sum((same & (down < across)).astype(I32), axis=0, keepdims=True)

    def slot_of(source, rank):
        outer, inner = source // p.rest, source % p.rest
        g, h = outer // p.copies, outer % p.copies
        return ((g * p.rest + inner) * p.copies + h) * capacity + rank

    seat_t[...] = onehot(slot_of(mine, rank_row) == iota((p.slots, tubes), 0))

    wait(5)
    wait(4)
    for matrix in range(p.matrices):
        rows = slice(matrix * p.points, (matrix + 1) * p.points)
        weights_out[rows, :] = dot(weights[matrix], reorder[...]).astype(BF)


def lane_masks(plan, rows):
    group = iota((rows, plan.half), 1) // plan.levels
    return [group == index for index in range(plan.fields)]


def pack_masks(plan):
    member = iota((plan.unit, plan.half), 0) // plan.lon_pad
    return [member == index for index in range(plan.pack)]


def chosen(masks, pieces):
    result = pieces[0]
    for mask, piece in zip(masks[1:], pieces[1:]):
        result = jnp.where(mask, piece, result)
    return result


def rolled(plan, array, groups):
    groups = groups % plan.fields
    if groups == 0:
        return array
    return pltpu.roll(array, groups * plan.levels, axis=1)


def neutral_kernel(plan, wait, arrived, table, weights, pick_t, out, wide, blocks, outcomes):
    p = plan
    for part in range(2):
        wide[part * p.rows_sent : (part + 1) * p.rows_sent, :] = arrived[
            :, part * p.half : (part + 1) * p.half
        ].astype(F32)
    stacks = []
    for lat in range(p.lat_held):
        parts = [
            wide[strided_rows(p, part, lat, wave), :]
            for part in range(2)
            for wave in range(p.wave_local)
        ]
        stacks.append(jnp.concatenate(parts, 0).astype(BF))
    spectra = jnp.concatenate(stacks, 1)
    spectra = jnp.concatenate([spectra, spectra], 0)
    grid = dot(table[...], spectra) * p.waves ** (-0.5)
    masks = lane_masks(p, p.cells)
    members = pack_masks(p)
    per = p.fields
    for copy in range(p.copies):
        for step in range(p.width // per):
            pieces = []
            for index in range(per):
                start = (step * per + index) * p.unit
                packs = []
                for pack in range(0, p.lat_local, p.pack):
                    lats = [copy * p.lat_local + pack + member for member in range(p.pack)]
                    parts = [
                        grid[start : start + p.unit, lat * p.half : (lat + 1) * p.half]
                        for lat in lats
                    ]
                    packs.append(chosen(members, parts))
                pieces.append(jnp.concatenate(packs, 0))
            for field in range(p.fields):
                turned = [rolled(p, pieces[index], index - field) for index in range(per)]
                first = (copy * p.fields + field) * p.cells
                blocks[first : first + p.cells, step * p.half : (step + 1) * p.half] = (
                    chosen(masks, turned).astype(BF)
                )
    values = blocks[...]
    for matrix in range(p.matrices):
        part = weights[matrix * p.points : (matrix + 1) * p.points, :]
        found = dot_nt(values, part).astype(BF)
        for copy in range(p.copies):
            for field in range(p.fields):
                first = (copy * p.fields + field) * p.cells
                outcomes[
                    copy,
                    matrix * p.cells : (matrix + 1) * p.cells,
                    field * p.points : (field + 1) * p.points,
                ] = found[first : first + p.cells, :]
    for copy in range(p.copies):
        taken = dot_tn(pick_t[copy], outcomes[copy]).astype(BF)
        out[:, copy] = taken.reshape(p.members, p.capacity, p.values)


def tube_kernel(
    plan, wait, arrived, seat_t, tube_state, collision, inverse, state_out, out, drag, held, done
):
    neutral = dot_tn(seat_t[...], arrived[...])
    copies = []
    for field in range(plan.fields):
        lanes = slice(field * plan.points, (field + 1) * plan.points)
        wind = neutral[:, lanes]
        force_high, force_low = split(tube_state[field] + wind)
        inverse_high, inverse_low = split(inverse[field])
        state = dot_nt(force_high, inverse_high) + (
            dot_nt(force_high, inverse_low) + dot_nt(force_low, inverse_high)
        )
        held[field] = state
        copies.append(
            pltpu.make_async_copy(held.at[field], state_out.at[field], done.at[field])
        )
        copies[-1].start()
        drag[:, lanes] = (collision[...] * (state - wind)).astype(BF)
    out[...] = dot(seat_t[...], drag[...]).astype(BF)
    for copy in copies:
        copy.wait()


def tendency_kernel(plan, wait, arrived, table, weights, pick_t, out, sums, spread, wide):
    p = plan
    for copy in range(p.copies):
        taken = arrived[:, copy].reshape(p.slots_held, p.values)
        found = dot(pick_t[copy], taken).astype(BF)
        for matrix in range(p.matrices):
            for field in range(p.fields):
                first = (copy * p.fields + field) * p.cells
                sums[
                    first : first + p.cells, matrix * p.points : (matrix + 1) * p.points
                ] = found[
                    matrix * p.cells : (matrix + 1) * p.cells,
                    field * p.points : (field + 1) * p.points,
                ]
    tendency = dot(sums[...], weights[...])
    masks = lane_masks(p, p.cells)
    members = pack_masks(p)
    per = p.fields
    for copy in range(p.copies):
        for step in range(p.width // per):
            pieces = []
            for field in range(p.fields):
                first = (copy * p.fields + field) * p.cells
                pieces.append(
                    tendency[first : first + p.cells, step * p.half : (step + 1) * p.half]
                )
            for index in range(per):
                turned = [rolled(p, pieces[field], field - index) for field in range(p.fields)]
                mixed = chosen(masks, turned)
                start = (step * per + index) * p.unit
                for lat in range(p.lat_local):
                    held = copy * p.lat_local + lat
                    pack, member = lat // p.pack, lat % p.pack
                    rows = mixed[pack * p.unit : (pack + 1) * p.unit, :]
                    spread[start : start + p.unit, held * p.half : (held + 1) * p.half] = (
                        jnp.where(members[member], rows, 0.0) if p.pack > 1 else rows
                    )
    high, low = split(spread[...])
    analysed = dot(table[...], jnp.concatenate([high, high, low], 0)) * LON ** (-0.5)
    for lat in range(p.lat_held):
        for part in range(2):
            for wave in range(p.wave_local):
                start = (part * p.wave_local + wave) * p.sources
                wide[strided_rows(p, part, lat, wave), :] = analysed[
                    start : start + p.sources, lat * p.half : (lat + 1) * p.half
                ]
    for part in range(2):
        out[:, part * p.half : (part + 1) * p.half] = wide[
            part * p.rows_sent : (part + 1) * p.rows_sent, :
        ].astype(BF)


def analysis_kernel(plan, wait, arrived, rows, order, analysis, spectral, out):
    joined = arrived[:, 0].astype(F32)
    for copy in range(1, plan.copies):
        joined = joined + arrived[:, copy].astype(F32)
    joined = joined.reshape(plan.rows, plan.columns).astype(BF)
    natural = dot_tn(rows[...], joined).astype(BF)
    natural = dot_nt(natural, order[...]).astype(BF)
    for wave in range(plan.wave_local):
        part = natural[wave * plan.latitudes : (wave + 1) * plan.latitudes, :]
        out[wave] = spectral[wave].astype(F32) + dot(analysis[wave], part)


def call(
    plan, kernel, outs, operands, scratch=(), smem=0, fetched=(), late=(), stored=(), flops=0
):
    vmem = pl.BlockSpec(memory_space=pltpu.VMEM)
    hbm = pl.BlockSpec(memory_space=pltpu.HBM)
    scalar = pl.BlockSpec(memory_space=pltpu.SMEM)
    in_specs = [
        scalar if i < smem else hbm if i in fetched else vmem for i in range(len(operands))
    ]
    size = sum(math.prod(o.shape) * o.dtype.itemsize for o in operands)
    operands = [
        pltpu.with_memory_space_constraint(o, pltpu.HBM) if i in fetched else o
        for i, o in enumerate(operands)
    ]
    held = [pltpu.VMEM(s, d) for s, d in scratch]
    for i in stored:
        held += [pltpu.VMEM(*outs[i]), pltpu.SemaphoreType.DMA(outs[i][0][:1])]
    if fetched:
        held += [pltpu.VMEM(operands[i].shape, operands[i].dtype) for i in fetched]
        held += [pltpu.SemaphoreType.DMA((len(fetched),))]

    def body(*refs):
        refs = list(refs)
        copies = {}
        for place, i in enumerate(fetched):
            target = refs[place - 1 - len(fetched)]
            copies[i] = pltpu.make_async_copy(refs[i], target, refs[-1].at[place])
            copies[i].start()
        for place, i in enumerate(fetched):
            refs[i] = refs[place - 1 - len(fetched)]
        for i in fetched:
            if i not in late:
                copies[i].wait()
        if fetched:
            refs = refs[: -1 - len(fetched)]
        kernel(plan, lambda i: copies[i].wait(), *refs)

    return pl.pallas_call(
        body,
        out_shape=[jax.ShapeDtypeStruct(s, d) for s, d in outs],
        in_specs=in_specs,
        out_specs=[hbm if i in stored else vmem for i in range(len(outs))],
        scratch_shapes=held,
        cost_estimate=pl.CostEstimate(flops=flops, bytes_accessed=size, transcendentals=0),
        compiler_params=pltpu.CompilerParams(vmem_limit_bytes=VMEM_LIMIT),
        name=kernel.__name__,
    )(*operands)


def swept(plan, neutral, tube_state, end_coupling, block_inverse):
    highest = lax.Precision.HIGHEST
    count = lax.axis_size("lev")
    wind = neutral.reshape(plan.tubes, plan.fields, plan.points).transpose(1, 0, 2)

    def solve(vector):
        return jnp.einsum("fpq,ftq->ftp", block_inverse, vector, precision=highest)

    forcing = tube_state + wind
    state = solve(forcing)
    for _ in range(SWEEPS):
        from_left = lax.ppermute(state[:, :, -1], "lev", [(i, i + 1) for i in range(count - 1)])
        from_right = lax.ppermute(state[:, :, 0], "lev", [(i + 1, i) for i in range(count - 1)])
        coupled = forcing.at[:, :, 0].add(end_coupling * from_left)
        coupled = coupled.at[:, :, -1].add(end_coupling * from_right)
        state = solve(coupled)
    return state, wind


def on_device(
    spectral,
    synthesis,
    analysis,
    interp_weights,
    tube_source,
    tube_column,
    weight_ids,
    tube_state,
    collision,
    end_coupling,
    block_inverse,
):
    plan = Plan(
        *[lax.axis_size(axis) for axis in ALL],
        spectral.shape,
        synthesis.shape,
        interp_weights.shape,
        tube_state.shape,
    )
    p = plan
    me = jnp.stack([lax.axis_index(axis) for axis in ALL]).astype(I32)
    lanes = math.gcd(p.tubes, 128)
    by_lane = (p.sources * p.tubes // lanes, lanes)
    forward_table, backward_table = fourier_tables(p)
    order = column_order(p)
    wave_order = chosen_rows(wave_rows(p), p.rows)

    (sent,) = call(
        p,
        synthesis_kernel,
        [((p.grp, p.copies, p.rows // p.grp, p.columns), BF)],
        (spectral, synthesis.transpose(0, 2, 1), order, wave_order),
        fetched=(0, 1, 2, 3),
    )
    flat = (p.rows_sent, p.columns)
    fourier = exchange(sent.reshape(flat), ALL, p.sources)
    weights, pick_t, seat_t = call(
        p,
        routing_kernel,
        [
            ((p.matrices * p.points, p.block), BF),
            ((p.copies, p.table, p.slots_held), BF),
            ((p.slots, p.tubes), BF),
        ],
        (
            me,
            tube_source.reshape(by_lane),
            tube_column.reshape(by_lane),
            weight_ids.reshape(by_lane),
            interp_weights,
            block_order(p),
        ),
        smem=1,
        fetched=(1, 2, 3, 5, 4),
        late=(4, 5),
        flops=1 << 31,
    )
    by_slot = (p.members, p.copies, p.capacity, p.values)
    flat = (p.slots, p.values)
    (sent,) = call(
        p,
        neutral_kernel,
        [(by_slot, BF)],
        (fourier, forward_table, weights, pick_t),
        scratch=[
            ((2 * p.rows_sent, p.half), F32),
            ((p.copies * p.fields * p.cells, p.block), BF),
            ((p.copies, p.table, p.values), BF),
        ],
    )
    arrived = exchange(sent.reshape(flat), GROUP, p.members)
    if lax.axis_size("lev") == 1:
        state, sent = call(
            p,
            tube_kernel,
            [(tube_state.shape, F32), (flat, BF)],
            (arrived, seat_t, tube_state, collision, block_inverse),
            scratch=[((p.tubes, p.values), BF)],
            stored=(0,),
        )
    else:
        state, wind = swept(p, dot_tn(seat_t, arrived), tube_state, end_coupling, block_inverse)
        drag = (collision[None, :, :] * (state - wind)).astype(BF)
        drag = drag.transpose(1, 0, 2).reshape(p.tubes, p.values)
        sent = dot(seat_t, drag).astype(BF)
    contrib = exchange(sent, GROUP, p.members)
    (sent,) = call(
        p,
        tendency_kernel,
        [((p.rows_sent, p.columns), BF)],
        (
            contrib.reshape(by_slot),
            backward_table,
            weights,
            pick_t,
        ),
        scratch=[
            ((p.copies * p.fields * p.cells, p.matrices * p.points), BF),
            ((p.width * p.unit, p.lat_held * p.half), F32),
            ((2 * p.rows_sent, p.half), F32),
        ],
    )
    analysed = exchange(sent, ALL, p.sources)
    (spectral_new,) = call(
        p,
        analysis_kernel,
        [(spectral.shape, F32)],
        (
            analysed.reshape(p.grp, p.copies, p.rows // p.grp, p.columns),
            wave_order,
            order,
            analysis,
            spectral,
        ),
    )
    return spectral_new, state


def solution(mesh):
    grp, band, lev = (mesh.shape[axis] for axis in ("grp", "band", "lev"))
    copies = 2 if band % 2 == 0 else 1
    parts = mesh.devices.reshape(grp, copies, band // copies, lev)
    mesh = Mesh(parts, ("grp", "hold", "rest", "lev"))
    placed = (
        P(ALL, None, "lev"),
        P(ALL, None, None),
        P(ALL, None, None),
        P(),
        P(),
        P(),
        P(),
        P(None, ALL, "lev"),
        P(ALL, "lev"),
        P(None, ALL),
        P(None, "lev", None),
    )
    return jax.shard_map(
        on_device,
        mesh=mesh,
        in_specs=placed,
        out_specs=(P(ALL, None, "lev"), P(None, ALL, "lev")),
        check_vma=False,
    )
```

```python
import math

import jax
import jax.numpy as jnp
import numpy as np
from jax import lax
from jax.experimental import pallas as pl
from jax.experimental.pallas import tpu as pltpu
from jax.sharding import Mesh
from jax.sharding import PartitionSpec as P

LON = 192
SWEEPS = 4
BF = jnp.bfloat16
F32 = jnp.float32
I32 = jnp.int32
ALL = ("grp", "hold", "rest")
GROUP = ("grp", "rest")
VMEM_LIMIT = 24 << 20


def dot(a, b):
    return jnp.dot(a, b, preferred_element_type=F32)


def dot_nt(a, b):
    return lax.dot_general(a, b, (((1,), (1,)), ((), ())), preferred_element_type=F32)


def dot_tn(a, b):
    return lax.dot_general(a, b, (((0,), (0,)), ((), ())), preferred_element_type=F32)


def split(x):
    high = x.astype(BF)
    return high, (x - high.astype(F32)).astype(BF)


def iota(shape, dim):
    return lax.broadcasted_iota(I32, shape, dim)


def onehot(mask):
    return mask.astype(F32).astype(BF)


class Plan:
    def __init__(self, grp, copies, rest, spectral, synthesis, weights, tube_state):
        self.grp, self.copies, self.rest = grp, copies, rest
        self.sources = grp * copies * rest
        self.members = grp * rest
        self.wave_local, self.latitudes, self.degrees = synthesis
        self.waves = self.wave_local * self.sources
        self.lat_local = self.latitudes // self.sources
        self.lat_held = self.lat_local * copies
        self.columns = spectral[2]
        self.fields, self.tubes, self.points = tube_state
        self.matrices, _, self.block = weights
        self.levels = self.columns // (2 * self.fields)
        self.width = self.block // self.levels
        self.lon_blocks = LON // self.width
        fits = [
            n
            for n in range(1, self.lat_local + 1)
            if self.lat_local % n == 0 and n * self.lon_blocks % 8 == 0
        ]
        self.pack = fits[0] if fits else 1
        self.lon_pad = self.lon_blocks if fits else -(-self.lon_blocks // 8) * 8
        self.unit = self.pack * self.lon_pad
        self.capacity = 2 * self.tubes // self.sources
        self.slots = self.sources * self.capacity
        self.slots_held = self.members * self.capacity
        self.rows = self.wave_local * self.latitudes
        self.rows_sent = self.rows * copies
        self.cells = self.lat_local * self.lon_pad
        self.table = self.matrices * self.cells
        self.values = self.fields * self.points
        self.half = self.fields * self.levels


def chosen_rows(origin, count):
    origin = np.asarray(origin).reshape(-1)
    return jnp.asarray((origin[:, None] == np.arange(count)[None, :]).astype(BF))


def column_order(plan):
    natural = np.arange(plan.columns).reshape(plan.levels, plan.fields, 2)
    return chosen_rows(natural.transpose(2, 1, 0), plan.columns).T


def block_order(plan):
    natural = np.arange(plan.block).reshape(plan.levels, plan.width)
    return chosen_rows(natural.T, plan.block).T


def wave_rows(plan):
    p = plan
    index = np.arange(p.rows).reshape(p.wave_local, p.grp, p.copies, p.rest, p.lat_local)
    return index.transpose(1, 3, 2, 0, 4)


def strided_rows(plan, part, lat, wave):
    copy, local = lat // plan.lat_local, lat % plan.lat_local
    start = (copy * plan.wave_local + wave) * plan.lat_local + local + part * plan.rows_sent
    return pl.ds(start, plan.sources, stride=plan.copies * plan.wave_local * plan.lat_local)


def fourier_tables(plan):
    wave = np.arange(plan.waves).reshape(plan.sources, plan.wave_local).T.reshape(-1)
    lon = np.arange(LON)
    angle = 2.0 * math.pi * ((wave[:, None] * lon[None, :]) % LON) / LON
    full = np.stack([np.cos(angle), -np.sin(angle)], 0)
    full = full.reshape(2, plan.waves, plan.lon_blocks, plan.width)
    full = np.pad(full, ((0, 0), (0, 0), (0, plan.lon_pad - plan.lon_blocks), (0, 0)))
    forward = full.transpose(3, 2, 0, 1)[:, None]
    forward = np.broadcast_to(forward, (plan.width, plan.pack) + forward.shape[2:])
    forward = forward.reshape(plan.width * plan.unit, 2 * plan.waves)
    high = forward.astype(BF)
    low = (forward - high.astype(np.float64)).astype(BF)
    synthesis = np.concatenate([high, low], 1)
    analysis = np.concatenate([high.T, low.T, high.T], 1)
    return jnp.asarray(synthesis), jnp.asarray(analysis)


def exchange(array, axes, count):
    shaped = array.reshape(count, array.shape[0] // count, array.shape[1])
    moved = lax.all_to_all(shaped, axes, split_axis=0, concat_axis=0, tiled=True)
    return moved.reshape(array.shape)


def synthesis_kernel(plan, wait, spectral, synthesis_t, out):
    p = plan
    column = iota((1, p.columns), 1)
    part, rest = column // p.half, column % p.half
    origin = ((rest % p.levels) * p.fields + rest // p.levels) * 2 + part
    order = onehot(iota((p.columns, p.columns), 0) == origin)
    row = iota((p.rows, 1), 0)
    local, row = row % p.lat_local, row // p.lat_local
    owner, row = row % p.wave_local, row // p.wave_local
    copy, row = row % p.copies, row // p.copies
    rest, group = row % p.rest, row // p.rest
    latitude = ((group * p.copies + copy) * p.rest + rest) * p.lat_local + local
    places = []
    for wave in range(p.wave_local):
        place = jnp.where(owner == wave, latitude, -1)
        places.append(onehot(iota((p.rows, p.latitudes), 1) == place))
    wait(0)
    wait(1)
    total = 0.0
    for wave in range(p.wave_local):
        moved = dot(spectral[wave], order).astype(BF)
        placed = dot_nt(places[wave], synthesis_t[wave]).astype(BF)
        total = total + dot(placed, moved)
    moved = total.astype(BF).reshape(p.grp, p.rows // p.grp, p.columns)
    for copy in range(p.copies):
        out[:, copy] = moved


def routing_kernel(
    plan,
    wait,
    me,
    owners,
    columns,
    weight_of,
    weights,
    reorder,
    weights_out,
    pick_t,
    seat_t,
):
    p = plan
    mine_g, mine_h, mine_l = me[0], me[1], me[2]
    tubes, capacity = p.tubes, p.capacity
    halves = owners.shape[0] // p.sources
    lanes = owners.shape[1]
    column = columns[...]
    cell = column
    for step in range(1, p.lat_local):
        late = (column >= step * p.lon_blocks).astype(I32)
        cell = cell + late * (p.lon_pad - p.lon_blocks)
    facts = [owners[...], cell + 1, weight_of[...]]
    facts = [fact.astype(F32).astype(BF) for fact in facts]

    def rows_of(fact, device):
        taken = []
        for half in range(halves):
            shape = (device.shape[0], p.sources * halves)
            taken.append(dot(onehot(device * halves + half == iota(shape, 1)), fact))
        return jnp.concatenate(taken, 1)

    member = iota((p.members, 1), 0)
    member_g, member_l = member // p.rest, member % p.rest
    device = (member_g * p.copies + mine_h) * p.rest + member_l
    owner, cell, matrix = [rows_of(fact, device) for fact in facts]
    before = onehot(iota((tubes, tubes), 0) < iota((tubes, tubes), 1))
    repeat = onehot(
        iota((p.slots_held, p.members), 0) // capacity == iota((p.slots_held, p.members), 1)
    )
    cell_all = dot(repeat, cell.astype(BF))
    matrix_all = dot(repeat, matrix.astype(BF))
    place = (iota((p.slots_held, tubes), 0) % capacity).astype(F32)
    ones = jnp.ones((16, tubes), BF)
    for copy in range(p.copies):
        source = ((mine_g * p.copies + copy) * p.rest + mine_l).astype(F32)
        mask = owner == source
        rank = jnp.where(mask, dot(onehot(mask), before), -1.0)
        taken = dot(repeat, rank.astype(BF)) == place
        cell_slot = jnp.where(taken, cell_all, 0.0)
        matrix_slot = jnp.where(taken, matrix_all, 0.0)
        row = dot_nt(ones, cell_slot.astype(BF)) + dot_nt(ones, matrix_slot.astype(BF)) * p.cells
        row = row[0:1, :].astype(I32) - 1
        pick_t[copy] = onehot(row == iota((p.table, p.slots_held), 0))

    myself = jnp.zeros((16, 1), I32) + ((mine_g * p.copies + mine_h) * p.rest + mine_l)
    mine = rows_of(facts[0], myself)[0:1, :].astype(I32)
    square = (tubes, tubes)
    down, across = iota(square, 0), iota(square, 1)
    mine_col = jnp.sum(jnp.where(down == across, mine, 0), axis=1, keepdims=True)
    same = mine_col == mine
    rank_row = jnp.sum((same & (down < across)).astype(I32), axis=0, keepdims=True)

    def slot_of(source, rank):
        outer, inner = source // p.rest, source % p.rest
        g, h = outer // p.copies, outer % p.copies
        return ((g * p.rest + inner) * p.copies + h) * capacity + rank

    seat_t[...] = onehot(slot_of(mine, rank_row) == iota((p.slots, tubes), 0))

    wait(5)
    wait(4)
    for matrix in range(p.matrices):
        rows = slice(matrix * p.points, (matrix + 1) * p.points)
        weights_out[rows, :] = dot(weights[matrix], reorder[...]).astype(BF)


def lane_masks(plan, rows):
    group = iota((rows, plan.half), 1) // plan.levels
    return [group == index for index in range(plan.fields)]


def pack_masks(plan):
    member = iota((plan.unit, plan.half), 0) // plan.lon_pad
    return [member == index for index in range(plan.pack)]


def chosen(masks, pieces):
    result = pieces[0]
    for mask, piece in zip(masks[1:], pieces[1:]):
        result = jnp.where(mask, piece, result)
    return result


def rolled(plan, array, groups):
    groups = groups % plan.fields
    if groups == 0:
        return array
    return pltpu.roll(array, groups * plan.levels, axis=1)


def neutral_kernel(plan, wait, arrived, table, weights, pick_t, out, wide, blocks, outcomes):
    p = plan
    for part in range(2):
        wide[part * p.rows_sent : (part + 1) * p.rows_sent, :] = arrived[
            :, part * p.half : (part + 1) * p.half
        ].astype(F32)
    stacks = []
    for lat in range(p.lat_held):
        parts = [
            wide[strided_rows(p, part, lat, wave), :]
            for part in range(2)
            for wave in range(p.wave_local)
        ]
        stacks.append(jnp.concatenate(parts, 0).astype(BF))
    spectra = jnp.concatenate(stacks, 1)
    spectra = jnp.concatenate([spectra, spectra], 0)
    grid = dot(table[...], spectra) * p.waves ** (-0.5)
    masks = lane_masks(p, p.cells)
    members = pack_masks(p)
    per = p.fields
    for copy in range(p.copies):
        for step in range(p.width // per):
            pieces = []
            for index in range(per):
                start = (step * per + index) * p.unit
                packs = []
                for pack in range(0, p.lat_local, p.pack):
                    lats = [copy * p.lat_local + pack + member for member in range(p.pack)]
                    parts = [
                        grid[start : start + p.unit, lat * p.half : (lat + 1) * p.half]
                        for lat in lats
                    ]
                    packs.append(chosen(members, parts))
                pieces.append(jnp.concatenate(packs, 0))
            for field in range(p.fields):
                turned = [rolled(p, pieces[index], index - field) for index in range(per)]
                first = (copy * p.fields + field) * p.cells
                blocks[first : first + p.cells, step * p.half : (step + 1) * p.half] = (
                    chosen(masks, turned).astype(BF)
                )
    values = blocks[...]
    for matrix in range(p.matrices):
        part = weights[matrix * p.points : (matrix + 1) * p.points, :]
        found = dot_nt(values, part).astype(BF)
        for copy in range(p.copies):
            for field in range(p.fields):
                first = (copy * p.fields + field) * p.cells
                outcomes[
                    copy,
                    matrix * p.cells : (matrix + 1) * p.cells,
                    field * p.points : (field + 1) * p.points,
                ] = found[first : first + p.cells, :]
    for copy in range(p.copies):
        taken = dot_tn(pick_t[copy], outcomes[copy]).astype(BF)
        out[:, copy] = taken.reshape(p.members, p.capacity, p.values)


def tube_kernel(
    plan, wait, arrived, seat_t, tube_state, collision, inverse, state_out, out, drag, held, done
):
    neutral = dot_tn(seat_t[...], arrived[...])
    copies = []
    for field in range(plan.fields):
        lanes = slice(field * plan.points, (field + 1) * plan.points)
        wind = neutral[:, lanes]
        force_high, force_low = split(tube_state[field] + wind)
        inverse_high, inverse_low = split(inverse[field])
        state = dot_nt(force_high, inverse_high) + (
            dot_nt(force_high, inverse_low) + dot_nt(force_low, inverse_high)
        )
        held[field] = state
        copies.append(
            pltpu.make_async_copy(held.at[field], state_out.at[field], done.at[field])
        )
        copies[-1].start()
        drag[:, lanes] = (collision[...] * (state - wind)).astype(BF)
    out[...] = dot(seat_t[...], drag[...]).astype(BF)
    for copy in copies:
        copy.wait()


def tendency_kernel(plan, wait, arrived, table, weights, pick_t, out, sums, spread, wide):
    p = plan
    for copy in range(p.copies):
        taken = arrived[:, copy].reshape(p.slots_held, p.values)
        found = dot(pick_t[copy], taken).astype(BF)
        for matrix in range(p.matrices):
            for field in range(p.fields):
                first = (copy * p.fields + field) * p.cells
                sums[
                    first : first + p.cells, matrix * p.points : (matrix + 1) * p.points
                ] = found[
                    matrix * p.cells : (matrix + 1) * p.cells,
                    field * p.points : (field + 1) * p.points,
                ]
    masks = lane_masks(p, p.cells)
    members = pack_masks(p)
    per = p.fields
    steps = p.width // per
    group = math.gcd(steps, 2)
    for step in range(steps):
        if step % group == 0:
            tendency = dot(sums[...], weights[:, step * p.half : (step + group) * p.half])
        lanes = slice(step % group * p.half, (step % group + 1) * p.half)
        for copy in range(p.copies):
            pieces = []
            for field in range(p.fields):
                first = (copy * p.fields + field) * p.cells
                pieces.append(tendency[first : first + p.cells, lanes])
            for index in range(per):
                turned = [rolled(p, pieces[field], field - index) for field in range(p.fields)]
                mixed = chosen(masks, turned)
                start = (step * per + index) * p.unit
                for lat in range(p.lat_local):
                    held = copy * p.lat_local + lat
                    pack, member = lat // p.pack, lat % p.pack
                    rows = mixed[pack * p.unit : (pack + 1) * p.unit, :]
                    spread[start : start + p.unit, held * p.half : (held + 1) * p.half] = (
                        jnp.where(members[member], rows, 0.0) if p.pack > 1 else rows
                    )
    high, low = split(spread[...])
    analysed = dot(table[...], jnp.concatenate([high, high, low], 0)) * LON ** (-0.5)
    for lat in range(p.lat_held):
        for part in range(2):
            for wave in range(p.wave_local):
                start = (part * p.wave_local + wave) * p.sources
                wide[strided_rows(p, part, lat, wave), :] = analysed[
                    start : start + p.sources, lat * p.half : (lat + 1) * p.half
                ]
    for part in range(2):
        out[:, part * p.half : (part + 1) * p.half] = wide[
            part * p.rows_sent : (part + 1) * p.rows_sent, :
        ].astype(BF)


def analysis_kernel(plan, wait, arrived, rows, order, analysis, spectral, out, held, done):
    p = plan
    placed = []
    for wave in range(p.wave_local):
        here = rows[:, wave * p.latitudes : (wave + 1) * p.latitudes]
        placed.append(dot_nt(analysis[wave], here).astype(BF))
    joined = arrived[:, 0].astype(F32)
    for copy in range(1, p.copies):
        joined = joined + arrived[:, copy].astype(F32)
    joined = joined.reshape(p.rows, p.columns).astype(BF)
    natural = dot_nt(joined, order[...]).astype(BF)
    copies = []
    for wave in range(p.wave_local):
        held[wave] = spectral[wave].astype(F32) + dot(placed[wave], natural)
        copies.append(pltpu.make_async_copy(held.at[wave], out.at[wave], done.at[wave]))
        copies[-1].start()
    for copy in copies:
        copy.wait()


def call(
    plan, kernel, outs, operands, scratch=(), smem=0, fetched=(), late=(), stored=(), flops=0
):
    vmem = pl.BlockSpec(memory_space=pltpu.VMEM)
    hbm = pl.BlockSpec(memory_space=pltpu.HBM)
    scalar = pl.BlockSpec(memory_space=pltpu.SMEM)
    in_specs = [
        scalar if i < smem else hbm if i in fetched else vmem for i in range(len(operands))
    ]
    size = sum(math.prod(o.shape) * o.dtype.itemsize for o in operands)
    operands = [
        pltpu.with_memory_space_constraint(o, pltpu.HBM) if i in fetched else o
        for i, o in enumerate(operands)
    ]
    held = [pltpu.VMEM(s, d) for s, d in scratch]
    for i in stored:
        held += [pltpu.VMEM(*outs[i]), pltpu.SemaphoreType.DMA(outs[i][0][:1])]
    if fetched:
        held += [pltpu.VMEM(operands[i].shape, operands[i].dtype) for i in fetched]
        held += [pltpu.SemaphoreType.DMA((len(fetched),))]

    def body(*refs):
        refs = list(refs)
        copies = {}
        for place, i in enumerate(fetched):
            target = refs[place - 1 - len(fetched)]
            copies[i] = pltpu.make_async_copy(refs[i], target, refs[-1].at[place])
            copies[i].start()
        for place, i in enumerate(fetched):
            refs[i] = refs[place - 1 - len(fetched)]
        for i in fetched:
            if i not in late:
                copies[i].wait()
        if fetched:
            refs = refs[: -1 - len(fetched)]
        kernel(plan, lambda i: copies[i].wait(), *refs)

    return pl.pallas_call(
        body,
        out_shape=[jax.ShapeDtypeStruct(s, d) for s, d in outs],
        in_specs=in_specs,
        out_specs=[hbm if i in stored else vmem for i in range(len(outs))],
        scratch_shapes=held,
        cost_estimate=pl.CostEstimate(flops=flops, bytes_accessed=size, transcendentals=0),
        compiler_params=pltpu.CompilerParams(vmem_limit_bytes=VMEM_LIMIT),
        name=kernel.__name__,
    )(*operands)


def swept(plan, neutral, tube_state, end_coupling, block_inverse):
    highest = lax.Precision.HIGHEST
    count = lax.axis_size("lev")
    wind = neutral.reshape(plan.tubes, plan.fields, plan.points).transpose(1, 0, 2)

    def solve(vector):
        return jnp.einsum("fpq,ftq->ftp", block_inverse, vector, precision=highest)

    forcing = tube_state + wind
    state = solve(forcing)
    for _ in range(SWEEPS):
        from_left = lax.ppermute(state[:, :, -1], "lev", [(i, i + 1) for i in range(count - 1)])
        from_right = lax.ppermute(state[:, :, 0], "lev", [(i + 1, i) for i in range(count - 1)])
        coupled = forcing.at[:, :, 0].add(end_coupling * from_left)
        coupled = coupled.at[:, :, -1].add(end_coupling * from_right)
        state = solve(coupled)
    return state, wind


def on_device(
    spectral,
    synthesis,
    analysis,
    interp_weights,
    tube_source,
    tube_column,
    weight_ids,
    tube_state,
    collision,
    end_coupling,
    block_inverse,
):
    plan = Plan(
        *[lax.axis_size(axis) for axis in ALL],
        spectral.shape,
        synthesis.shape,
        interp_weights.shape,
        tube_state.shape,
    )
    p = plan
    me = jnp.stack([lax.axis_index(axis) for axis in ALL]).astype(I32)
    lanes = math.gcd(p.tubes, 128)
    by_lane = (p.sources * p.tubes // lanes, lanes)
    forward_table, backward_table = fourier_tables(p)
    order = column_order(p)
    wave_order = chosen_rows(wave_rows(p), p.rows)

    (sent,) = call(
        p,
        synthesis_kernel,
        [((p.grp, p.copies, p.rows // p.grp, p.columns), BF)],
        (spectral, synthesis.transpose(0, 2, 1)),
        fetched=(0, 1),
        late=(0, 1),
    )
    flat = (p.rows_sent, p.columns)
    fourier = exchange(sent.reshape(flat), ALL, p.sources)
    weights, pick_t, seat_t = call(
        p,
        routing_kernel,
        [
            ((p.matrices * p.points, p.block), BF),
            ((p.copies, p.table, p.slots_held), BF),
            ((p.slots, p.tubes), BF),
        ],
        (
            me,
            tube_source.reshape(by_lane),
            tube_column.reshape(by_lane),
            weight_ids.reshape(by_lane),
            interp_weights,
            block_order(p),
        ),
        smem=1,
        fetched=(1, 2, 3, 5, 4),
        late=(4, 5),
        flops=1 << 31,
    )
    by_slot = (p.members, p.copies, p.capacity, p.values)
    flat = (p.slots, p.values)
    (sent,) = call(
        p,
        neutral_kernel,
        [(by_slot, BF)],
        (fourier, forward_table, weights, pick_t),
        scratch=[
            ((2 * p.rows_sent, p.half), F32),
            ((p.copies * p.fields * p.cells, p.block), BF),
            ((p.copies, p.table, p.values), BF),
        ],
    )
    arrived = exchange(sent.reshape(flat), GROUP, p.members)
    if lax.axis_size("lev") == 1:
        state, sent = call(
            p,
            tube_kernel,
            [(tube_state.shape, F32), (flat, BF)],
            (arrived, seat_t, tube_state, collision, block_inverse),
            scratch=[((p.tubes, p.values), BF)],
            stored=(0,),
        )
    else:
        state, wind = swept(p, dot_tn(seat_t, arrived), tube_state, end_coupling, block_inverse)
        drag = (collision[None, :, :] * (state - wind)).astype(BF)
        drag = drag.transpose(1, 0, 2).reshape(p.tubes, p.values)
        sent = dot(seat_t, drag).astype(BF)
    contrib = exchange(sent, GROUP, p.members)
    (sent,) = call(
        p,
        tendency_kernel,
        [((p.rows_sent, p.columns), BF)],
        (
            contrib.reshape(by_slot),
            backward_table,
            weights,
            pick_t,
        ),
        scratch=[
            ((p.copies * p.fields * p.cells, p.matrices * p.points), BF),
            ((p.width * p.unit, p.lat_held * p.half), F32),
            ((2 * p.rows_sent, p.half), F32),
        ],
    )
    analysed = exchange(sent, ALL, p.sources)
    (spectral_new,) = call(
        p,
        analysis_kernel,
        [(spectral.shape, F32)],
        (
            analysed.reshape(p.grp, p.copies, p.rows // p.grp, p.columns),
            wave_order,
            order,
            analysis,
            spectral,
        ),
        stored=(0,),
    )
    return spectral_new, state


def solution(mesh):
    grp, band, lev = (mesh.shape[axis] for axis in ("grp", "band", "lev"))
    copies = 2 if band % 2 == 0 else 1
    parts = mesh.devices.reshape(grp, copies, band // copies, lev)
    mesh = Mesh(parts, ("grp", "hold", "rest", "lev"))
    placed = (
        P(ALL, None, "lev"),
        P(ALL, None, None),
        P(ALL, None, None),
        P(),
        P(),
        P(),
        P(),
        P(None, ALL, "lev"),
        P(ALL, "lev"),
        P(None, ALL),
        P(None, "lev", None),
    )
    return jax.shard_map(
        on_device,
        mesh=mesh,
        in_specs=placed,
        out_specs=(P(ALL, None, "lev"), P(None, ALL, "lev")),
        check_vma=False,
    )
```

```python
import math

import jax
import jax.numpy as jnp
import numpy as np
from jax import lax
from jax.experimental import pallas as pl
from jax.experimental.pallas import tpu as pltpu
from jax.sharding import Mesh
from jax.sharding import PartitionSpec as P

LON = 192
SWEEPS = 4
BF = jnp.bfloat16
F32 = jnp.float32
I32 = jnp.int32
ALL = ("grp", "hold", "rest")
GROUP = ("grp", "rest")
VMEM_LIMIT = 24 << 20


def dot(a, b):
    return jnp.dot(a, b, preferred_element_type=F32)


def dot_nt(a, b):
    return lax.dot_general(a, b, (((1,), (1,)), ((), ())), preferred_element_type=F32)


def dot_tn(a, b):
    return lax.dot_general(a, b, (((0,), (0,)), ((), ())), preferred_element_type=F32)


def split(x):
    high = x.astype(BF)
    return high, (x - high.astype(F32)).astype(BF)


def iota(shape, dim):
    return lax.broadcasted_iota(I32, shape, dim)


def onehot(mask):
    return mask.astype(F32).astype(BF)


class Plan:
    def __init__(self, grp, copies, rest, spectral, synthesis, weights, tube_state):
        self.grp, self.copies, self.rest = grp, copies, rest
        self.sources = grp * copies * rest
        self.members = grp * rest
        self.wave_local, self.latitudes, self.degrees = synthesis
        self.waves = self.wave_local * self.sources
        self.lat_local = self.latitudes // self.sources
        self.lat_held = self.lat_local * copies
        self.columns = spectral[2]
        self.fields, self.tubes, self.points = tube_state
        self.matrices, _, self.block = weights
        self.levels = self.columns // (2 * self.fields)
        self.width = self.block // self.levels
        self.lon_blocks = LON // self.width
        fits = [
            n
            for n in range(1, self.lat_local + 1)
            if self.lat_local % n == 0 and n * self.lon_blocks % 8 == 0
        ]
        self.pack = fits[0] if fits else 1
        self.lon_pad = self.lon_blocks if fits else -(-self.lon_blocks // 8) * 8
        self.unit = self.pack * self.lon_pad
        self.capacity = 2 * self.tubes // self.sources
        self.slots = self.sources * self.capacity
        self.slots_held = self.members * self.capacity
        self.rows = self.wave_local * self.latitudes
        self.rows_sent = self.rows * copies
        self.cells = self.lat_local * self.lon_pad
        self.table = self.matrices * self.cells
        self.values = self.fields * self.points
        self.half = self.fields * self.levels


def chosen_rows(origin, count):
    origin = np.asarray(origin).reshape(-1)
    return jnp.asarray((origin[:, None] == np.arange(count)[None, :]).astype(BF))


def column_order(plan):
    natural = np.arange(plan.columns).reshape(plan.levels, plan.fields, 2)
    return chosen_rows(natural.transpose(2, 1, 0), plan.columns).T


def block_order(plan):
    natural = np.arange(plan.block).reshape(plan.levels, plan.width)
    return chosen_rows(natural.T, plan.block).T


def wave_rows(plan):
    p = plan
    index = np.arange(p.rows).reshape(p.wave_local, p.grp, p.copies, p.rest, p.lat_local)
    return index.transpose(1, 3, 2, 0, 4)


def strided_rows(plan, part, lat, wave):
    copy, local = lat // plan.lat_local, lat % plan.lat_local
    start = (copy * plan.wave_local + wave) * plan.lat_local + local + part * plan.rows_sent
    return pl.ds(start, plan.sources, stride=plan.copies * plan.wave_local * plan.lat_local)


def fourier_tables(plan):
    wave = np.arange(plan.waves).reshape(plan.sources, plan.wave_local).T.reshape(-1)
    lon = np.arange(LON)
    angle = 2.0 * math.pi * ((wave[:, None] * lon[None, :]) % LON) / LON
    full = np.stack([np.cos(angle), -np.sin(angle)], 0)
    full = full.reshape(2, plan.waves, plan.lon_blocks, plan.width)
    full = np.pad(full, ((0, 0), (0, 0), (0, plan.lon_pad - plan.lon_blocks), (0, 0)))
    forward = full.transpose(3, 2, 0, 1)[:, None]
    forward = np.broadcast_to(forward, (plan.width, plan.pack) + forward.shape[2:])
    forward = forward.reshape(plan.width * plan.unit, 2 * plan.waves)
    high = forward.astype(BF)
    low = (forward - high.astype(np.float64)).astype(BF)
    synthesis = np.concatenate([high, low], 1)
    analysis = np.concatenate([high.T, low.T, high.T], 1)
    return jnp.asarray(synthesis), jnp.asarray(analysis)


def exchange(array, axes, count):
    shaped = array.reshape(count, array.shape[0] // count, array.shape[1])
    moved = lax.all_to_all(shaped, axes, split_axis=0, concat_axis=0, tiled=True)
    return moved.reshape(array.shape)


def synthesis_kernel(plan, wait, spectral, synthesis_t, out):
    p = plan
    column = iota((1, p.columns), 1)
    part, rest = column // p.half, column % p.half
    origin = ((rest % p.levels) * p.fields + rest // p.levels) * 2 + part
    order = onehot(iota((p.columns, p.columns), 0) == origin)
    row = iota((p.rows, 1), 0)
    local, row = row % p.lat_local, row // p.lat_local
    owner, row = row % p.wave_local, row // p.wave_local
    copy, row = row % p.copies, row // p.copies
    rest, group = row % p.rest, row // p.rest
    latitude = ((group * p.copies + copy) * p.rest + rest) * p.lat_local + local
    places = []
    for wave in range(p.wave_local):
        place = jnp.where(owner == wave, latitude, -1)
        places.append(onehot(iota((p.rows, p.latitudes), 1) == place))
    wait(0)
    wait(1)
    total = 0.0
    for wave in range(p.wave_local):
        moved = dot(spectral[wave], order).astype(BF)
        placed = dot_nt(places[wave], synthesis_t[wave]).astype(BF)
        total = total + dot(placed, moved)
    moved = total.astype(BF).reshape(p.grp, p.rows // p.grp, p.columns)
    for copy in range(p.copies):
        out[:, copy] = moved


def routing_kernel(
    plan,
    wait,
    me,
    owners,
    columns,
    weight_of,
    weights,
    reorder,
    weights_out,
    pick_t,
    seat_t,
):
    p = plan
    mine_g, mine_h, mine_l = me[0], me[1], me[2]
    tubes, capacity = p.tubes, p.capacity
    halves = owners.shape[0] // p.sources
    lanes = owners.shape[1]
    column = columns[...]
    cell = column
    for step in range(1, p.lat_local):
        late = (column >= step * p.lon_blocks).astype(I32)
        cell = cell + late * (p.lon_pad - p.lon_blocks)
    facts = [owners[...], cell + 1, weight_of[...]]
    facts = [fact.astype(F32).astype(BF) for fact in facts]

    def rows_of(fact, device):
        taken = []
        for half in range(halves):
            shape = (device.shape[0], p.sources * halves)
            taken.append(dot(onehot(device * halves + half == iota(shape, 1)), fact))
        return jnp.concatenate(taken, 1)

    member = iota((p.members, 1), 0)
    member_g, member_l = member // p.rest, member % p.rest
    device = (member_g * p.copies + mine_h) * p.rest + member_l
    owner, cell, matrix = [rows_of(fact, device) for fact in facts]
    before = onehot(iota((tubes, tubes), 0) < iota((tubes, tubes), 1))
    repeat = onehot(
        iota((p.slots_held, p.members), 0) // capacity == iota((p.slots_held, p.members), 1)
    )
    cell_all = dot(repeat, cell.astype(BF))
    matrix_all = dot(repeat, matrix.astype(BF))
    place = (iota((p.slots_held, tubes), 0) % capacity).astype(F32)
    ones = jnp.ones((16, tubes), BF)
    for copy in range(p.copies):
        source = ((mine_g * p.copies + copy) * p.rest + mine_l).astype(F32)
        mask = owner == source
        rank = jnp.where(mask, dot(onehot(mask), before), -1.0)
        taken = dot(repeat, rank.astype(BF)) == place
        cell_slot = jnp.where(taken, cell_all, 0.0)
        matrix_slot = jnp.where(taken, matrix_all, 0.0)
        row = dot_nt(ones, cell_slot.astype(BF)) + dot_nt(ones, matrix_slot.astype(BF)) * p.cells
        row = row[0:1, :].astype(I32) - 1
        pick_t[copy] = onehot(row == iota((p.table, p.slots_held), 0))

    myself = jnp.zeros((16, 1), I32) + ((mine_g * p.copies + mine_h) * p.rest + mine_l)
    mine = rows_of(facts[0], myself)[0:1, :].astype(I32)
    square = (tubes, tubes)
    down, across = iota(square, 0), iota(square, 1)
    mine_col = jnp.sum(jnp.where(down == across, mine, 0), axis=1, keepdims=True)
    same = mine_col == mine
    rank_row = jnp.sum((same & (down < across)).astype(I32), axis=0, keepdims=True)

    def slot_of(source, rank):
        outer, inner = source // p.rest, source % p.rest
        g, h = outer // p.copies, outer % p.copies
        return ((g * p.rest + inner) * p.copies + h) * capacity + rank

    seat_t[...] = onehot(slot_of(mine, rank_row) == iota((p.slots, tubes), 0))

    wait(5)
    wait(4)
    for matrix in range(p.matrices):
        rows = slice(matrix * p.points, (matrix + 1) * p.points)
        weights_out[rows, :] = dot(weights[matrix], reorder[...]).astype(BF)


def lane_masks(plan, rows):
    group = iota((rows, plan.half), 1) // plan.levels
    return [group == index for index in range(plan.fields)]


def pack_masks(plan):
    member = iota((plan.unit, plan.half), 0) // plan.lon_pad
    return [member == index for index in range(plan.pack)]


def chosen(masks, pieces):
    result = pieces[0]
    for mask, piece in zip(masks[1:], pieces[1:]):
        result = jnp.where(mask, piece, result)
    return result


def rolled(plan, array, groups):
    groups = groups % plan.fields
    if groups == 0:
        return array
    return pltpu.roll(array, groups * plan.levels, axis=1)


def neutral_kernel(plan, wait, arrived, table, weights, pick_t, out, wide, blocks, outcomes):
    p = plan
    for part in range(2):
        wide[part * p.rows_sent : (part + 1) * p.rows_sent, :] = arrived[
            :, part * p.half : (part + 1) * p.half
        ].astype(F32)
    stacks = []
    for lat in range(p.lat_held):
        parts = [
            wide[strided_rows(p, part, lat, wave), :]
            for part in range(2)
            for wave in range(p.wave_local)
        ]
        stacks.append(jnp.concatenate(parts, 0).astype(BF))
    spectra = jnp.concatenate(stacks, 1)
    spectra = jnp.concatenate([spectra, spectra], 0)
    grid = dot(table[...], spectra) * p.waves ** (-0.5)
    masks = lane_masks(p, p.cells)
    members = pack_masks(p)
    per = p.fields
    for copy in range(p.copies):
        for step in range(p.width // per):
            pieces = []
            for index in range(per):
                start = (step * per + index) * p.unit
                packs = []
                for pack in range(0, p.lat_local, p.pack):
                    lats = [copy * p.lat_local + pack + member for member in range(p.pack)]
                    parts = [
                        grid[start : start + p.unit, lat * p.half : (lat + 1) * p.half]
                        for lat in lats
                    ]
                    packs.append(chosen(members, parts))
                pieces.append(jnp.concatenate(packs, 0))
            for field in range(p.fields):
                turned = [rolled(p, pieces[index], index - field) for index in range(per)]
                first = (copy * p.fields + field) * p.cells
                blocks[first : first + p.cells, step * p.half : (step + 1) * p.half] = (
                    chosen(masks, turned).astype(BF)
                )
    values = blocks[...]
    for matrix in range(p.matrices):
        part = weights[matrix * p.points : (matrix + 1) * p.points, :]
        found = dot_nt(values, part).astype(BF)
        for copy in range(p.copies):
            for field in range(p.fields):
                first = (copy * p.fields + field) * p.cells
                outcomes[
                    copy,
                    matrix * p.cells : (matrix + 1) * p.cells,
                    field * p.points : (field + 1) * p.points,
                ] = found[first : first + p.cells, :]
    for copy in range(p.copies):
        taken = dot_tn(pick_t[copy], outcomes[copy]).astype(BF)
        out[:, copy] = taken.reshape(p.members, p.capacity, p.values)


def tube_kernel(
    plan, wait, arrived, seat_t, tube_state, collision, inverse, state_out, out, drag
):
    neutral = dot_tn(seat_t[...], arrived[...])
    for field in range(plan.fields):
        lanes = slice(field * plan.points, (field + 1) * plan.points)
        wind = neutral[:, lanes]
        force_high, force_low = split(tube_state[field] + wind)
        inverse_high, inverse_low = split(inverse[field])
        state = dot_nt(force_high, inverse_high) + (
            dot_nt(force_high, inverse_low) + dot_nt(force_low, inverse_high)
        )
        state_out[field] = state
        drag[:, lanes] = (collision[...] * (state - wind)).astype(BF)
    out[...] = dot(seat_t[...], drag[...]).astype(BF)


def tendency_kernel(
    plan, wait, arrived, table, weights, pick_t, state, out, state_out, sums, spread, wide, done
):
    p = plan
    store = pltpu.make_async_copy(state, state_out, done)
    store.start()
    for copy in range(p.copies):
        taken = arrived[:, copy].reshape(p.slots_held, p.values)
        found = dot(pick_t[copy], taken).astype(BF)
        for matrix in range(p.matrices):
            for field in range(p.fields):
                first = (copy * p.fields + field) * p.cells
                sums[
                    first : first + p.cells, matrix * p.points : (matrix + 1) * p.points
                ] = found[
                    matrix * p.cells : (matrix + 1) * p.cells,
                    field * p.points : (field + 1) * p.points,
                ]
    masks = lane_masks(p, p.cells)
    members = pack_masks(p)
    per = p.fields
    steps = p.width // per
    group = math.gcd(steps, 2)
    for step in range(steps):
        if step % group == 0:
            tendency = dot(sums[...], weights[:, step * p.half : (step + group) * p.half])
        lanes = slice(step % group * p.half, (step % group + 1) * p.half)
        for copy in range(p.copies):
            pieces = []
            for field in range(p.fields):
                first = (copy * p.fields + field) * p.cells
                pieces.append(tendency[first : first + p.cells, lanes])
            for index in range(per):
                turned = [rolled(p, pieces[field], field - index) for field in range(p.fields)]
                mixed = chosen(masks, turned)
                start = (step * per + index) * p.unit
                for lat in range(p.lat_local):
                    held = copy * p.lat_local + lat
                    pack, member = lat // p.pack, lat % p.pack
                    rows = mixed[pack * p.unit : (pack + 1) * p.unit, :]
                    spread[start : start + p.unit, held * p.half : (held + 1) * p.half] = (
                        jnp.where(members[member], rows, 0.0) if p.pack > 1 else rows
                    )
    high, low = split(spread[...])
    analysed = dot(table[...], jnp.concatenate([high, high, low], 0)) * LON ** (-0.5)
    for lat in range(p.lat_held):
        for part in range(2):
            for wave in range(p.wave_local):
                start = (part * p.wave_local + wave) * p.sources
                wide[strided_rows(p, part, lat, wave), :] = analysed[
                    start : start + p.sources, lat * p.half : (lat + 1) * p.half
                ]
    for part in range(2):
        out[:, part * p.half : (part + 1) * p.half] = wide[
            part * p.rows_sent : (part + 1) * p.rows_sent, :
        ].astype(BF)
    store.wait()


def analysis_kernel(plan, wait, arrived, rows, order, analysis, spectral, out, held, done):
    p = plan
    placed = []
    for wave in range(p.wave_local):
        here = rows[:, wave * p.latitudes : (wave + 1) * p.latitudes]
        placed.append(dot_nt(analysis[wave], here).astype(BF))
    joined = arrived[:, 0].astype(F32)
    for copy in range(1, p.copies):
        joined = joined + arrived[:, copy].astype(F32)
    joined = joined.reshape(p.rows, p.columns).astype(BF)
    natural = dot_nt(joined, order[...]).astype(BF)
    copies = []
    for wave in range(p.wave_local):
        held[wave] = spectral[wave].astype(F32) + dot(placed[wave], natural)
        copies.append(pltpu.make_async_copy(held.at[wave], out.at[wave], done.at[wave]))
        copies[-1].start()
    for copy in copies:
        copy.wait()


def call(
    plan, kernel, outs, operands, scratch=(), smem=0, fetched=(), late=(), stored=(), handed=(), flops=0
):
    vmem = pl.BlockSpec(memory_space=pltpu.VMEM)
    hbm = pl.BlockSpec(memory_space=pltpu.HBM)
    scalar = pl.BlockSpec(memory_space=pltpu.SMEM)
    in_specs = [
        scalar if i < smem else hbm if i in fetched else vmem for i in range(len(operands))
    ]
    size = sum(math.prod(o.shape) * o.dtype.itemsize for o in operands)
    operands = [
        pltpu.with_memory_space_constraint(o, pltpu.HBM) if i in fetched else o
        for i, o in enumerate(operands)
    ]
    held = [pltpu.VMEM(s, d) for s, d in scratch]
    for i in stored:
        held += [pltpu.VMEM(*outs[i]), pltpu.SemaphoreType.DMA(outs[i][0][:1])]
    if handed:
        held += [pltpu.SemaphoreType.DMA(())]
    if fetched:
        held += [pltpu.VMEM(operands[i].shape, operands[i].dtype) for i in fetched]
        held += [pltpu.SemaphoreType.DMA((len(fetched),))]

    def body(*refs):
        refs = list(refs)
        copies = {}
        for place, i in enumerate(fetched):
            target = refs[place - 1 - len(fetched)]
            copies[i] = pltpu.make_async_copy(refs[i], target, refs[-1].at[place])
            copies[i].start()
        for place, i in enumerate(fetched):
            refs[i] = refs[place - 1 - len(fetched)]
        for i in fetched:
            if i not in late:
                copies[i].wait()
        if fetched:
            refs = refs[: -1 - len(fetched)]
        kernel(plan, lambda i: copies[i].wait(), *refs)

    return pl.pallas_call(
        body,
        out_shape=[jax.ShapeDtypeStruct(s, d) for s, d in outs],
        in_specs=in_specs,
        out_specs=[hbm if i in stored + handed else vmem for i in range(len(outs))],
        scratch_shapes=held,
        cost_estimate=pl.CostEstimate(flops=flops, bytes_accessed=size, transcendentals=0),
        compiler_params=pltpu.CompilerParams(vmem_limit_bytes=VMEM_LIMIT),
        name=kernel.__name__,
    )(*operands)


def swept(plan, neutral, tube_state, end_coupling, block_inverse):
    highest = lax.Precision.HIGHEST
    count = lax.axis_size("lev")
    wind = neutral.reshape(plan.tubes, plan.fields, plan.points).transpose(1, 0, 2)

    def solve(vector):
        return jnp.einsum("fpq,ftq->ftp", block_inverse, vector, precision=highest)

    forcing = tube_state + wind
    state = solve(forcing)
    for _ in range(SWEEPS):
        from_left = lax.ppermute(state[:, :, -1], "lev", [(i, i + 1) for i in range(count - 1)])
        from_right = lax.ppermute(state[:, :, 0], "lev", [(i + 1, i) for i in range(count - 1)])
        coupled = forcing.at[:, :, 0].add(end_coupling * from_left)
        coupled = coupled.at[:, :, -1].add(end_coupling * from_right)
        state = solve(coupled)
    return state, wind


def on_device(
    spectral,
    synthesis,
    analysis,
    interp_weights,
    tube_source,
    tube_column,
    weight_ids,
    tube_state,
    collision,
    end_coupling,
    block_inverse,
):
    plan = Plan(
        *[lax.axis_size(axis) for axis in ALL],
        spectral.shape,
        synthesis.shape,
        interp_weights.shape,
        tube_state.shape,
    )
    p = plan
    me = jnp.stack([lax.axis_index(axis) for axis in ALL]).astype(I32)
    lanes = math.gcd(p.tubes, 128)
    by_lane = (p.sources * p.tubes // lanes, lanes)
    forward_table, backward_table = fourier_tables(p)
    order = column_order(p)
    wave_order = chosen_rows(wave_rows(p), p.rows)

    (sent,) = call(
        p,
        synthesis_kernel,
        [((p.grp, p.copies, p.rows // p.grp, p.columns), BF)],
        (spectral, synthesis.transpose(0, 2, 1)),
        fetched=(0, 1),
        late=(0, 1),
    )
    flat = (p.rows_sent, p.columns)
    fourier = exchange(sent.reshape(flat), ALL, p.sources)
    weights, pick_t, seat_t = call(
        p,
        routing_kernel,
        [
            ((p.matrices * p.points, p.block), BF),
            ((p.copies, p.table, p.slots_held), BF),
            ((p.slots, p.tubes), BF),
        ],
        (
            me,
            tube_source.reshape(by_lane),
            tube_column.reshape(by_lane),
            weight_ids.reshape(by_lane),
            interp_weights,
            block_order(p),
        ),
        smem=1,
        fetched=(1, 2, 3, 5, 4),
        late=(4, 5),
        flops=1 << 31,
    )
    by_slot = (p.members, p.copies, p.capacity, p.values)
    flat = (p.slots, p.values)
    (sent,) = call(
        p,
        neutral_kernel,
        [(by_slot, BF)],
        (fourier, forward_table, weights, pick_t),
        scratch=[
            ((2 * p.rows_sent, p.half), F32),
            ((p.copies * p.fields * p.cells, p.block), BF),
            ((p.copies, p.table, p.values), BF),
        ],
    )
    arrived = exchange(sent.reshape(flat), GROUP, p.members)
    if lax.axis_size("lev") == 1:
        state, sent = call(
            p,
            tube_kernel,
            [(tube_state.shape, F32), (flat, BF)],
            (arrived, seat_t, tube_state, collision, block_inverse),
            scratch=[((p.tubes, p.values), BF)],
        )
    else:
        state, wind = swept(p, dot_tn(seat_t, arrived), tube_state, end_coupling, block_inverse)
        drag = (collision[None, :, :] * (state - wind)).astype(BF)
        drag = drag.transpose(1, 0, 2).reshape(p.tubes, p.values)
        sent = dot(seat_t, drag).astype(BF)
    contrib = exchange(sent, GROUP, p.members)
    sent, state = call(
        p,
        tendency_kernel,
        [((p.rows_sent, p.columns), BF), (state.shape, F32)],
        (
            contrib.reshape(by_slot),
            backward_table,
            weights,
            pick_t,
            state,
        ),
        scratch=[
            ((p.copies * p.fields * p.cells, p.matrices * p.points), BF),
            ((p.width * p.unit, p.lat_held * p.half), F32),
            ((2 * p.rows_sent, p.half), F32),
        ],
        handed=(1,),
    )
    analysed = exchange(sent, ALL, p.sources)
    (spectral_new,) = call(
        p,
        analysis_kernel,
        [(spectral.shape, F32)],
        (
            analysed.reshape(p.grp, p.copies, p.rows // p.grp, p.columns),
            wave_order,
            order,
            analysis,
            spectral,
        ),
        stored=(0,),
    )
    return spectral_new, state


def solution(mesh):
    grp, band, lev = (mesh.shape[axis] for axis in ("grp", "band", "lev"))
    copies = 2 if band % 2 == 0 else 1
    parts = mesh.devices.reshape(grp, copies, band // copies, lev)
    mesh = Mesh(parts, ("grp", "hold", "rest", "lev"))
    placed = (
        P(ALL, None, "lev"),
        P(ALL, None, None),
        P(ALL, None, None),
        P(),
        P(),
        P(),
        P(),
        P(None, ALL, "lev"),
        P(ALL, "lev"),
        P(None, ALL),
        P(None, "lev", None),
    )
    return jax.shard_map(
        on_device,
        mesh=mesh,
        in_specs=placed,
        out_specs=(P(ALL, None, "lev"), P(None, ALL, "lev")),
        check_vma=False,
    )
```
